128 devices in a mesh: req: 16 (over y_hi, x, core), head: 8 (over y_lo, z).
Axes of the slice: x: 4, y: 4 (y_hi: 2, y_lo: 2; y = y_hi * 2 + y_lo), z: 4, core: 2. Of those that a mesh axis runs over, the one named last changes fastest.
Arguments:
- hidden: bfloat16 [512, 16, 2048], P('req', None, 'head'), may hold values from -6 to 6
- w_zx: bfloat16 [2048, 2, 4096], P(None, None, 'head'), may hold values from -0.125 to 0.125
- w_bc: bfloat16 [2048, 256], replicated, may hold values from -0.125 to 0.125
- w_dt: bfloat16 [2048, 64], P(None, 'head'), may hold values from -0.125 to 0.125
- conv_x_w: float32 [5, 4096], P(None, 'head'), may hold values from -3 to 3
- conv_bc_w: float32 [5, 256], replicated, may hold values from -3 to 3
- dt_bias: float32 [64], P('head'), may hold values from -4 to 0.5
- a_log: float32 [64], P('head'), may hold values from 0 to 2.5
- d_skip: float32 [64], P('head'), may hold values from 0.5 to 1.5
- norm_gain: float32 [4096], P('head'), may hold values from 0.1 to 1.9
- w_out: bfloat16 [4096, 2048], P('head'), may hold values from -0.09375 to 0.09375
- ssm_state: float32 [512, 64, 64, 128], P('req', 'head'), may hold values from -3 to 3
- conv_x_state: float32 [512, 3, 4096], P('req', None, 'head'), may hold values from -6 to 6
- conv_bc_state: float32 [512, 3, 256], P('req'), may hold values from -6 to 6
- slot: int32 [512], replicated, may hold values from 0 to 511, as said below
- lengths: int32 [512], replicated, may hold values from 0 to 16
- accepted: int32 [512], replicated, may hold values from 0 to 16
Outputs:
- out: bfloat16 [512, 16, 2048], P('req', None, 'head')
- new_state: float32 [512, 64, 64, 128], P('req', 'head')
- new_conv_x: float32 [512, 3, 4096], P('req', None, 'head')
- new_conv_bc: float32 [512, 3, 256], P('req')
The draws below stay inside these ranges and needn't reach their ends.
Inputs may be any that keep to these rules, and one draw needn't show every extreme that they name: slot is a permutation of the pool rows; the requests of each aligned block of 32 requests have exactly 2 pool rows in each aligned block of 32 pool rows.
All inputs are finite; a program needn't handle non-finite values.
Results may differ from the reference program's by a relative error of at most 0.0082.
Values may be sent and summed in bfloat16 or wider, within the bound.
No kernel may reach another device: no remote copies, remote signals or barrier semaphores. Data moves between devices by JAX's collectives and lax.ppermute only.
A program may use at most 128 MiB of HBM per device.

```python
import math
import jax
import jax.numpy as jnp
from jax import lax

D = 2048
H = 64
P_SIZE = 64
N = 128
K = 4
L = 16
REQ_DEV = 32
DI = 4096
REQUESTS = 512


def draw_slot(key, part):
    blocks = REQUESTS // REQ_DEV
    per_peer = REQ_DEV // blocks
    owner_key, request_key = jax.random.split(jax.random.fold_in(key, 7))
    owner_perm = jax.vmap(lambda sub: jax.random.permutation(sub, REQ_DEV))(jax.random.split(owner_key, blocks))
    request_perm = jax.vmap(lambda sub: jax.random.permutation(sub, REQ_DEV))(jax.random.split(request_key, blocks))
    places = jnp.arange(REQ_DEV, dtype=jnp.int32)
    owners = places // per_peer
    within = places % per_peer
    block_ids = jnp.arange(blocks, dtype=jnp.int32)
    columns = block_ids[:, None] * per_peer + within[None, :]
    values = owners[None, :] * REQ_DEV + owner_perm[owners[None, :], columns].astype(jnp.int32)
    targets = block_ids[:, None] * REQ_DEV + request_perm.astype(jnp.int32)
    return jnp.zeros((REQUESTS,), jnp.int32).at[targets.reshape(-1)].set(values.reshape(-1))


def with_ends(array, stream_key, smallest, top_value):
    place = [jax.random.randint(jax.random.fold_in(stream_key, axis), (), 0, length) for axis, length in enumerate(array.shape)]
    widest = array.shape.index(max(array.shape))
    neighbour = place[:widest] + [(place[widest] + 1) % array.shape[widest]] + place[widest + 1:]
    return array.at[tuple(place)].set(smallest).at[tuple(neighbour)].set(top_value)


def levels(key, shape, pieces, smallest, top_value):
    factor_of, own = 1.0, jax.random.fold_in(key, 6)
    for axis_at, parts in pieces:
        steps = jnp.exp(jax.random.uniform(jax.random.fold_in(own, axis_at), (parts,), jnp.float32, smallest / len(pieces), top_value / len(pieces)))
        factor_of = factor_of * jnp.repeat(steps, shape[axis_at] // parts).reshape([-1 if axis == axis_at else 1 for axis in range(len(shape))])
    return factor_of


def bell_draw(own_key, shape, scale, most, cuts=(), kind=jnp.bfloat16):
    array = jax.random.normal(own_key, shape, jnp.float32) * scale
    if len(cuts) > 0:
        array = levels(own_key, shape, cuts, -0.22, 0.18) * array
    return jnp.clip(array, min=-most, max=most).astype(kind)


def setup_inputs(seed: int = 0) -> dict:
    key_of = jax.random.split(jax.random.key(seed), 18)
    hidden = bell_draw(key_of[0], (REQUESTS, L, D), 1.0, 6.0, ((0, 16), (2, 8)))
    w_zx = bell_draw(key_of[1], (D, 2, DI), D ** -0.5, 0.125, ((2, 8),))
    w_bc = bell_draw(key_of[2], (D, 2 * N), D ** -0.5, 0.125)
    w_dt = bell_draw(key_of[3], (D, H), D ** -0.5, 0.125, ((1, 8),))
    conv_x_w = bell_draw(key_of[4], (K + 1, DI), 0.5, 3.0, ((1, 8),), jnp.float32)
    conv_bc_w = bell_draw(key_of[5], (K + 1, 2 * N), 0.5, 3.0, (), jnp.float32)
    dt_bias = jnp.clip(-4.0 + 4.5 * jax.random.uniform(key_of[6], (H,), jnp.float32) ** levels(key_of[6], (H,), ((0, 8),), -0.2, 0.2), -4.0, 0.5)
    a_log = jnp.clip(2.5 * jax.random.uniform(key_of[7], (H,), jnp.float32) ** levels(key_of[7], (H,), ((0, 8),), -0.2, 0.2), 0.0, 2.5)
    d_skip = jnp.clip(0.5 + 1.0 * jax.random.uniform(key_of[8], (H,), jnp.float32) ** levels(key_of[8], (H,), ((0, 8),), -0.2, 0.2), 0.5, 1.5)
    norm_gain = jnp.clip(1.0 + 0.18 * jax.random.normal(key_of[9], (DI,), jnp.float32), 0.1, 1.9)
    w_out = bell_draw(key_of[10], (DI, D), DI ** -0.5, 0.09375, ((0, 8),))
    ssm_state = bell_draw(key_of[11], (REQUESTS, H, P_SIZE, N), 0.3, 3.0, ((0, 16), (1, 8)), jnp.float32)
    conv_x_state = bell_draw(key_of[12], (REQUESTS, K - 1, DI), 1.0, 6.0, ((0, 16), (2, 8)), jnp.float32)
    conv_bc_state = bell_draw(key_of[13], (REQUESTS, K - 1, 2 * N), 1.0, 6.0, ((0, 16),), jnp.float32)
    slot = draw_slot(jax.random.fold_in(key_of[17], 71), 0)
    lengths = with_ends(jax.random.randint(key_of[15], (REQUESTS,), 0, L + 1), jax.random.fold_in(key_of[15], 1), 0, L).astype(jnp.int32)
    accepted = with_ends(jax.random.randint(key_of[16], (REQUESTS,), 0, L + 1), jax.random.fold_in(key_of[16], 1), 0, L).astype(jnp.int32)
    return dict(hidden=hidden, w_zx=w_zx, w_bc=w_bc, w_dt=w_dt, conv_x_w=conv_x_w, conv_bc_w=conv_bc_w, dt_bias=dt_bias, a_log=a_log, d_skip=d_skip, norm_gain=norm_gain, w_out=w_out, ssm_state=ssm_state, conv_x_state=conv_x_state, conv_bc_state=conv_bc_state, slot=slot, lengths=lengths, accepted=accepted)


highest = lax.Precision.HIGHEST

def conv_step(previous, inputs, taps):
    window = jnp.concatenate([previous, inputs.astype(jnp.float32)], axis=1)
    tail = taps.shape[0] - 1
    steps = inputs.shape[1]
    total = taps[tail] + taps[0] * window[:, 0:steps]
    for tap in range(1, tail):
        total = total + taps[tap] * window[:, tap:tap + steps]
    return (jax.nn.silu(total).astype(jnp.bfloat16), window)

def keep_rows(window, counted, tail):
    picks = counted[:, None] + jnp.arange(tail, dtype=jnp.int32)[None, :]
    return jnp.take_along_axis(window, picks[:, :, None], axis=1)

def scan_block(x_conv, bc_conv, dt_in, states, counted, dt_bias, a_log, d_skip):
    heads = states.shape[1]
    nstate = states.shape[3]
    blocks, steps, chans = x_conv.shape
    headdim = chans // heads
    xh = x_conv.astype(jnp.float32).reshape(blocks, steps, heads, headdim)
    bmat = bc_conv[..., :nstate].astype(jnp.float32)
    cmat = bc_conv[..., nstate:].astype(jnp.float32)
    step_size = jax.nn.softplus(dt_in.astype(jnp.float32) + dt_bias)
    rate = step_size * -jnp.exp(a_log)
    cumul = jnp.cumsum(rate, axis=1)
    carried = jnp.exp(cumul)[..., None] * jnp.einsum('bhpn,btn->bthp', states, cmat, precision=highest)
    inner = jnp.einsum('btn,bsn->bts', cmat, bmat, precision=highest)
    places = jnp.arange(steps, dtype=jnp.int32)
    lower = (places[:, None] >= places[None, :])[None, :, :, None]
    spread = cumul[:, :, None, :] - cumul[:, None, :, :]
    factor = jnp.where(lower, jnp.exp(jnp.where(lower, spread, 0.0)), 0.0)
    factor = factor * inner[..., None] * step_size[:, None, :, :]
    within = jnp.einsum('btsh,bshp->bthp', factor, xh, precision=highest)
    mixed = (carried + within + d_skip[:, None] * xh).reshape(blocks, steps, chans).astype(jnp.bfloat16)
    live = (places[None, :] < counted[:, None])[..., None]
    total = lax.optimization_barrier(jnp.sum(jnp.where(live, rate, 0.0), axis=1))
    remain = jnp.where(live, total[:, None, :] - cumul, 0.0)
    scaled = jnp.where(live, jnp.exp(remain) * step_size, 0.0)
    updated = jnp.exp(total)[:, :, None, None] * states
    updated = updated + jnp.einsum('bsh,bshp,bsn->bhpn', scaled, xh, bmat, precision=highest)
    return (mixed, updated)

def reference(hidden, w_zx, w_bc, w_dt, conv_x_w, conv_bc_w, dt_bias, a_log, d_skip, norm_gain, w_out, ssm_state, conv_x_state, conv_bc_state, slot, lengths, accepted):
    requests, steps, width = hidden.shape
    inner = w_zx.shape[2]
    bc_cols = w_bc.shape[1]
    tail = conv_x_state.shape[1]
    counted = jnp.minimum(accepted, lengths).astype(jnp.int32)
    holder = jnp.argsort(slot).astype(jnp.int32)
    stacked = jnp.concatenate([w_zx.reshape(width, 2 * inner), w_bc, w_dt], axis=1)
    group_size = math.gcd(requests, 16)

    def one_group(pool_rows):
        request_ids = holder[pool_rows]
        tokens = hidden[request_ids]
        projected = jnp.dot(tokens.reshape(-1, width), stacked, preferred_element_type=jnp.float32)
        projected = projected.astype(jnp.bfloat16).reshape(group_size, steps, -1)
        gate_in = projected[..., :inner]
        x_in = projected[..., inner:2 * inner]
        bc_in = projected[..., 2 * inner:2 * inner + bc_cols]
        dt_in = projected[..., 2 * inner + bc_cols:]
        mine = counted[request_ids]
        x_conv, x_window = conv_step(conv_x_state[pool_rows], x_in, conv_x_w)
        bc_conv, bc_window = conv_step(conv_bc_state[pool_rows], bc_in, conv_bc_w)
        mixed, updated = scan_block(x_conv, bc_conv, dt_in, ssm_state[pool_rows], mine, dt_bias, a_log, d_skip)
        gated = mixed.astype(jnp.float32) * jax.nn.silu(gate_in.astype(jnp.float32))
        meansq = lax.optimization_barrier(jnp.mean(gated * gated, axis=-1, keepdims=True))
        normed = (gated * lax.rsqrt(meansq + 1e-05) * norm_gain).astype(jnp.bfloat16)
        result = jnp.dot(normed.reshape(-1, inner), w_out, preferred_element_type=jnp.float32).reshape(group_size, steps, width)
        places = jnp.arange(steps, dtype=jnp.int32)
        valid = places[None, :] < lengths[request_ids][:, None]
        result = jnp.where(valid[..., None], result, 0.0).astype(jnp.bfloat16)
        return (result, updated, keep_rows(x_window, mine, tail), keep_rows(bc_window, mine, tail))
    pool_groups = jnp.arange(requests, dtype=jnp.int32).reshape(-1, group_size)
    out_pool, states_new, conv_x_new, conv_bc_new = lax.map(one_group, pool_groups)
    out_pool = out_pool.reshape(requests, steps, width)
    out = out_pool[slot]
    return (out, states_new.reshape(ssm_state.shape), conv_x_new.reshape(conv_x_state.shape), conv_bc_new.reshape(conv_bc_state.shape))
```

```python
import functools

import jax
import jax.numpy as jnp
from jax import lax
from jax.experimental import pallas as pl
from jax.experimental.pallas import tpu as pltpu
from jax.sharding import PartitionSpec as P

f32 = jnp.float32
bf16 = jnp.bfloat16
highest = lax.Precision.HIGHEST
NT = (((1,), (1,)), ((), ()))
TN = (((0,), (0,)), ((), ()))
STAT_ROWS = 8


def send_kernel(info, hid_ref, out_ref, seen, *, heads_dev):
    requests = hid_ref.shape[0]
    peers = seen.shape[0]
    for o in range(peers):
        seen[o] = 0

    def body(i, carry):
        owner = lax.div(info[i], requests)
        j = seen[owner]
        seen[owner] = j + 1
        rows = hid_ref[i]
        for h in range(heads_dev):
            out_ref[(owner * heads_dev + h) * 2 + j] = rows
        return carry

    lax.fori_loop(0, requests, body, 0)


def layer_kernel(
    arrive,
    recv_ref,
    wzx_ref,
    wbc_ref,
    wdt_ref,
    wout_ref,
    cxw_ref,
    cbw_ref,
    bias_ref,
    alog_ref,
    skip_ref,
    gain_ref,
    cvec_ref,
    cx_ref,
    cb_ref,
    state_hbm,
    out_ref,
    ncx_ref,
    ncb_ref,
    newstate_hbm,
    st_ref,
    xw_ref,
    bw_ref,
    gate_ref,
    dt_ref,
    ec_ref,
    sc_ref,
    fd_ref,
    dec_ref,
    g_ref,
    sq_ref,
    in_sem,
    out_sem,
    *,
    heads_dev,
):
    requests = cx_ref.shape[0]
    tail = cx_ref.shape[1]
    inner = xw_ref.shape[2]
    steps = recv_ref.shape[1]
    part = recv_ref.shape[2]
    peers = recv_ref.shape[0] // (2 * heads_dev)
    tokens = requests * steps
    nstate = st_ref.shape[2]
    heads = wdt_ref.shape[1]
    headdim = inner // heads
    spread = heads * steps
    base = 8 - tail
    blk = 256

    def load_state(i):
        return pltpu.make_async_copy(state_hbm.at[arrive[i]], st_ref.at[i], in_sem.at[i])

    def save_state(i):
        return pltpu.make_async_copy(st_ref.at[i], newstate_hbm.at[arrive[i]], out_sem.at[i])

    lax.fori_loop(0, requests, lambda i, c: (load_state(i).start(), c)[1], 0)

    view = recv_ref.reshape(peers, heads_dev, 2, steps, part)
    tok = jnp.concatenate(
        [view[:, h].reshape(tokens, part) for h in range(heads_dev)], axis=1
    )

    def proj(w):
        return jnp.dot(tok, w, preferred_element_type=f32).astype(bf16)

    for n in range(inner // blk):
        gate_ref[:, n * blk : (n + 1) * blk] = proj(wzx_ref[:, n * blk : (n + 1) * blk])
    for n in range(inner // blk):
        xw_ref[:, 8 : 8 + steps, n * blk : (n + 1) * blk] = (
            proj(wzx_ref[:, inner + n * blk : inner + (n + 1) * blk])
            .astype(f32)
            .reshape(requests, steps, blk)
        )
    bw_ref[:, 8 : 8 + steps, :] = proj(wbc_ref[...]).astype(f32).reshape(requests, steps, 2 * nstate)
    dt_in = proj(wdt_ref[...]).astype(f32)

    pre = dt_in + bias_ref[...]
    dt = jnp.maximum(pre, 0.0) + jnp.log1p(jnp.exp(-jnp.abs(pre)))
    rate = -dt * jnp.exp(alog_ref[...])
    place = lax.rem(lax.broadcasted_iota(jnp.int32, (tokens, heads), 0), steps)
    cumul = rate
    d = 1
    while d < steps:
        cumul = cumul + jnp.where(place >= d, pltpu.roll(cumul, d, 0), 0.0)
        d *= 2
    live = place < cvec_ref[...]
    total = jnp.sum(jnp.where(live, rate, 0.0).reshape(requests, steps, heads), axis=1, keepdims=True)
    dec_ref[...] = jnp.exp(total)
    totals = jnp.broadcast_to(total, (requests, steps, heads)).reshape(tokens, heads)
    scaled = jnp.where(live, jnp.exp(jnp.where(live, totals - cumul, 0.0)) * dt, 0.0)

    def pick(width, each):
        rows = lax.broadcasted_iota(jnp.int32, (heads, width), 0)
        cols = lax.div(lax.broadcasted_iota(jnp.int32, (heads, width), 1), each)
        return (rows == cols).astype(f32)

    to_chan = pick(inner, headdim)
    to_pair = pick(spread, steps)
    ec_ref[...] = jnp.dot(
        jnp.exp(cumul), to_chan, precision=highest, preferred_element_type=f32
    ).reshape(requests, steps, inner)
    sc_ref[...] = jnp.dot(
        scaled, to_chan, precision=highest, preferred_element_type=f32
    ).reshape(requests, steps, inner)
    cum2 = jnp.dot(cumul, to_pair, precision=highest, preferred_element_type=f32).reshape(
        requests, steps, spread
    )
    dt2 = jnp.dot(dt, to_pair, precision=highest, preferred_element_type=f32).reshape(
        requests, steps, spread
    )
    t_at = lax.broadcasted_iota(jnp.int32, (1, steps, spread), 1)
    s_at = lax.rem(lax.broadcasted_iota(jnp.int32, (1, steps, spread), 2), steps)
    same = t_at == s_at
    lower = t_at >= s_at
    crow = jnp.sum(jnp.where(same, cum2, 0.0), axis=1, keepdims=True)
    drow = jnp.sum(jnp.where(same, dt2, 0.0), axis=1, keepdims=True)
    fd_ref[...] = jnp.where(lower, jnp.exp(jnp.where(lower, cum2 - crow, 0.0)) * drow, 0.0)

    r_head = lax.div(lax.broadcasted_iota(jnp.int32, (spread, inner), 0), steps)
    c_head = lax.div(lax.broadcasted_iota(jnp.int32, (spread, inner), 1), headdim)
    diag = (r_head == c_head).astype(bf16)

    def conv(win_ref, w_ref, i):
        total_c = w_ref[tail + 1 : tail + 2, :]
        for k in range(tail + 1):
            total_c = total_c + w_ref[k : k + 1, :] * win_ref[i, base + k : base + k + steps, :]
        return (total_c * lax.logistic(total_c)).astype(bf16)

    def body(i, carry):
        row = arrive[i]
        count = arrive[requests + i]
        xw_ref[i, base:8, :] = cx_ref[row]
        bw_ref[i, base:8, :] = cb_ref[row]
        x = conv(xw_ref, cxw_ref, i)
        bc = conv(bw_ref, cbw_ref, i)
        back = 8 + steps - base - count
        ncx_ref[row] = pltpu.roll(xw_ref[i], back, 0)[:tail]
        ncb_ref[row] = pltpu.roll(bw_ref[i], back, 0)[:tail]
        b = bc[:, :nstate]
        c = bc[:, nstate:]
        load_state(i).wait()
        state = st_ref[i]
        carried = lax.dot_general(c, state.astype(bf16), NT, preferred_element_type=f32)
        many_b = jnp.concatenate([b] * heads, axis=0)
        gram = lax.dot_general(c, many_b, NT, preferred_element_type=f32)
        factor = (gram * fd_ref[i]).astype(bf16)
        many_x = jnp.concatenate([x] * heads, axis=0) * diag
        within = jnp.dot(factor, many_x, preferred_element_type=f32)
        xf = x.astype(f32)
        mixed = (carried * ec_ref[i] + within + skip_ref[...] * xf).astype(bf16)
        push = (xf * sc_ref[i]).astype(bf16)
        update = lax.dot_general(push, b, TN, preferred_element_type=f32)
        dec = dec_ref[i]
        for h in range(heads):
            sl = slice(h * headdim, (h + 1) * headdim)
            factor_h = jnp.broadcast_to(dec[:, h : h + 1], (headdim, nstate))
            st_ref[i, sl, :] = factor_h * state[sl, :] + update[sl, :]
        save_state(i).start()
        tok_at = pl.ds(pl.multiple_of(i * steps, steps), steps)
        gate = gate_ref[tok_at, :].astype(f32)
        gated = mixed.astype(f32) * (gate * lax.logistic(gate))
        sq_ref[tok_at, :] = (gated * gated).astype(bf16)
        g_ref[tok_at, :] = (gated * gain_ref[...]).astype(bf16)
        return carry

    lax.fori_loop(0, requests, body, 0)

    ones = jnp.ones((STAT_ROWS, inner), bf16)
    squares = lax.dot_general(ones, sq_ref[...], NT, preferred_element_type=f32)
    high = squares.astype(bf16).astype(f32)
    first = lax.broadcasted_iota(jnp.int32, squares.shape, 0) == 0
    stats = jnp.where(first, high, squares - high).astype(bf16)
    pair = 2 * steps
    data_rows = 2 * pair
    out_view = out_ref.reshape(peers, heads_dev, data_rows + STAT_ROWS, 128)
    for b in range(peers):
        piece = jnp.concatenate(
            [stats[:, b * pair : (b + 1) * pair], jnp.zeros((STAT_ROWS, 128 - pair), bf16)], axis=1
        )
        for h in range(heads_dev):
            out_view[b, h, data_rows:, :] = piece

    for h in range(heads_dev):
        res = jnp.dot(
            g_ref[...], wout_ref[:, h * part : (h + 1) * part], preferred_element_type=f32
        ).astype(bf16)
        out_view[:, h, 0:pair, :] = res[:, :128].reshape(peers, pair, 128)
        out_view[:, h, pair:data_rows, :] = res[:, 128:].reshape(peers, pair, 128)

    lax.fori_loop(0, requests, lambda i, c: (save_state(i).wait(), c)[1], 0)


def final_kernel(info, recv_ref, out_ref, seen, *, heads_dev, inner_all):
    requests, steps, part = out_ref.shape
    peers = seen.shape[0]
    pair = 2 * steps
    data_rows = 2 * pair
    for o in range(peers):
        seen[o] = 0
    view = recv_ref.reshape(peers, heads_dev, data_rows + STAT_ROWS, 128)
    eye = lax.broadcasted_iota(jnp.int32, (pair, 128), 0) == lax.broadcasted_iota(
        jnp.int32, (pair, 128), 1
    )
    place = lax.broadcasted_iota(jnp.int32, (steps, 128), 0)

    def body(i, carry):
        owner = lax.div(info[i], requests)
        length = info[requests + i]
        j = seen[owner]
        seen[owner] = j + 1
        stats = view[owner, 0, data_rows:, :].astype(f32)
        for h in range(1, heads_dev):
            stats = stats + view[owner, h, data_rows:, :].astype(f32)
        squares = stats[0:1, :] + stats[1:2, :]
        at = lax.broadcasted_iota(jnp.int32, (steps, 128), 0) + j * steps
        lane = lax.broadcasted_iota(jnp.int32, (steps, 128), 1)
        total = jnp.sum(jnp.where(lane == at, squares, 0.0), axis=1, keepdims=True)
        scale = lax.rsqrt(total / inner_all + 1e-05)
        keep = place < length
        for half in range(2):
            rows = pl.ds(pl.multiple_of(half * pair + j * steps, steps), steps)
            acc = view[owner, 0, rows, :].astype(f32)
            for h in range(1, heads_dev):
                acc = acc + view[owner, h, rows, :].astype(f32)
            out_ref[i, :, half * 128 : (half + 1) * 128] = jnp.where(keep, acc * scale, 0.0).astype(bf16)
        return carry

    lax.fori_loop(0, requests, body, 0)


def vmem(n):
    return [pl.BlockSpec(memory_space=pltpu.VMEM)] * n


def smem():
    return pl.BlockSpec(memory_space=pltpu.SMEM)


def any_space():
    return pl.BlockSpec(memory_space=pl.ANY)


def per_device(
    hidden,
    w_zx,
    w_bc,
    w_dt,
    conv_x_w,
    conv_bc_w,
    dt_bias,
    a_log,
    d_skip,
    norm_gain,
    w_out,
    ssm_state,
    conv_x_state,
    conv_bc_state,
    slot,
    lengths,
    accepted,
):
    requests, steps, part = hidden.shape
    width = w_zx.shape[0]
    inner = w_zx.shape[2]
    bc_cols = w_bc.shape[1]
    heads = w_dt.shape[1]
    headdim = inner // heads
    nstate = bc_cols // 2
    tail = conv_x_state.shape[1]
    peers = lax.axis_size("req")
    heads_dev = lax.axis_size("head")
    tokens = requests * steps
    spread = heads * steps
    out_rows = 4 * steps + STAT_ROWS
    me = lax.axis_index("req")

    slot_blocks = slot.reshape(peers, requests)
    mine = jnp.concatenate(
        [
            lax.dynamic_slice_in_dim(slot, me * requests, requests),
            lax.dynamic_slice_in_dim(lengths, me * requests, requests),
        ]
    )
    outgoing = pl.pallas_call(
        functools.partial(send_kernel, heads_dev=heads_dev),
        out_shape=jax.ShapeDtypeStruct((peers * heads_dev * 2, steps, part), bf16),
        in_specs=[smem()] + vmem(1),
        out_specs=vmem(1)[0],
        scratch_shapes=[pltpu.SMEM((peers,), jnp.int32)],
        name="send_rows",
    )(mine, hidden)
    arrived = lax.all_to_all(outgoing, ("req", "head"), split_axis=0, concat_axis=0, tiled=True)

    counted = jnp.minimum(accepted, lengths).reshape(peers, requests)
    order = jnp.arange(requests, dtype=jnp.int32)[None, :]
    code = (order * requests + slot_blocks % requests) * (2 * steps) + counted
    here = slot_blocks // requests == me
    low = jnp.min(jnp.where(here, code, jnp.iinfo(jnp.int32).max), axis=1)
    high = jnp.max(jnp.where(here, code, -1), axis=1)
    both = jnp.stack([low, high], axis=1).reshape(requests)
    rows = (both // (2 * steps)) % requests
    counts = both % (2 * steps)
    arrive = jnp.concatenate([rows, counts])
    count_col = jnp.broadcast_to(counts[:, None, None], (requests, steps, heads)).reshape(tokens, heads)

    leaving, new_conv_x, new_conv_bc, new_state = pl.pallas_call(
        functools.partial(layer_kernel, heads_dev=heads_dev),
        out_shape=(
            jax.ShapeDtypeStruct((peers * heads_dev, out_rows, 128), bf16),
            jax.ShapeDtypeStruct(conv_x_state.shape, f32),
            jax.ShapeDtypeStruct(conv_bc_state.shape, f32),
            jax.ShapeDtypeStruct((requests, inner, nstate), f32),
        ),
        in_specs=[smem()] + vmem(14) + [any_space()],
        out_specs=tuple(vmem(3)) + (any_space(),),
        scratch_shapes=[
            pltpu.VMEM((requests, inner, nstate), f32),
            pltpu.VMEM((requests, 8 + steps, inner), f32),
            pltpu.VMEM((requests, 8 + steps, bc_cols), f32),
            pltpu.VMEM((tokens, inner), bf16),
            pltpu.VMEM((tokens, heads), f32),
            pltpu.VMEM((requests, steps, inner), f32),
            pltpu.VMEM((requests, steps, inner), f32),
            pltpu.VMEM((requests, steps, spread), f32),
            pltpu.VMEM((requests, 1, heads), f32),
            pltpu.VMEM((tokens, inner), bf16),
            pltpu.VMEM((tokens, inner), bf16),
            pltpu.SemaphoreType.DMA((requests,)),
            pltpu.SemaphoreType.DMA((requests,)),
        ],
        compiler_params=pltpu.CompilerParams(vmem_limit_bytes=48 * 1024 * 1024),
        name="layer",
    )(
        arrive,
        arrived,
        w_zx.reshape(width, 2 * inner),
        w_bc,
        w_dt,
        w_out,
        conv_x_w,
        conv_bc_w,
        dt_bias[None, :],
        a_log[None, :],
        jnp.repeat(d_skip, headdim)[None, :],
        norm_gain[None, :],
        count_col,
        conv_x_state,
        conv_bc_state,
        ssm_state.reshape(requests, inner, nstate),
    )
    returned = lax.all_to_all(leaving, ("req", "head"), split_axis=0, concat_axis=0, tiled=True)
    out = pl.pallas_call(
        functools.partial(final_kernel, heads_dev=heads_dev, inner_all=inner * heads_dev),
        out_shape=jax.ShapeDtypeStruct((requests, steps, part), bf16),
        in_specs=[smem()] + vmem(1),
        out_specs=vmem(1)[0],
        scratch_shapes=[pltpu.SMEM((peers,), jnp.int32)],
        name="place_rows",
    )(mine, returned)
    return (out, new_state.reshape(ssm_state.shape), new_conv_x, new_conv_bc)


def solution(mesh):
    in_specs = (
        P("req", None, "head"),
        P(None, None, "head"),
        P(),
        P(None, "head"),
        P(None, "head"),
        P(),
        P("head"),
        P("head"),
        P("head"),
        P("head"),
        P("head", None),
        P("req", "head", None, None),
        P("req", None, "head"),
        P("req", None, None),
        P(),
        P(),
        P(),
    )
    out_specs = (
        P("req", None, "head"),
        P("req", "head", None, None),
        P("req", None, "head"),
        P("req", None, None),
    )
    return jax.shard_map(
        per_device, mesh=mesh, in_specs=in_specs, out_specs=out_specs, check_vma=False
    )
```

```python
import functools

import jax
import jax.numpy as jnp
from jax import lax
from jax.experimental import pallas as pl
from jax.experimental.pallas import tpu as pltpu
from jax.sharding import PartitionSpec as P

f32 = jnp.float32
bf16 = jnp.bfloat16
NT = (((1,), (1,)), ((), ()))
TN = (((0,), (0,)), ((), ()))
STAT_ROWS = 8
MIB = 1024 * 1024
MIX_MIB = 36
STAGE_MIB = 14
STATE_MIB = 16


def send_kernel(slot_ref, hid_ref, out_hbm, buf, seen, order, sem, *, heads_dev):
    requests = hid_ref.shape[0]
    peers = seen.shape[0]
    first = lax.axis_index("req") * requests
    for o in range(peers):
        seen[o] = 0

    def find(i, carry):
        owner = lax.div(slot_ref[first + i], requests)
        j = seen[owner]
        seen[owner] = j + 1
        order[owner * 2 + j] = i
        return carry

    lax.fori_loop(0, requests, find, 0, unroll=4)

    def block(o):
        at = pl.ds(o * 2 * heads_dev, 2 * heads_dev)
        return pltpu.make_async_copy(buf.at[at], out_hbm.at[at], sem.at[o])

    def fill(o, carry):
        for j in range(2):
            rows = hid_ref[order[o * 2 + j]]
            for h in range(heads_dev):
                buf[(o * heads_dev + h) * 2 + j] = rows
        block(o).start()
        return carry

    lax.fori_loop(0, peers, fill, 0, unroll=2)
    lax.fori_loop(0, peers, lambda o, c: (block(o).wait(), c)[1], 0)


def stage_kernel(arrive, state_hbm, turned_hbm, st_ref, turned_ref, in_sem, out_sem):
    requests = turned_ref.shape[0]

    def load_state(i):
        return pltpu.make_async_copy(state_hbm.at[arrive[i]], st_ref.at[i], in_sem.at[i])

    def save(i):
        return pltpu.make_async_copy(turned_ref.at[i], turned_hbm.at[i], out_sem.at[i])

    lax.fori_loop(0, requests, lambda i, c: (load_state(i).start(), c)[1], 0)

    def body(i, carry):
        load_state(i).wait()
        turned_ref[i] = st_ref[i].astype(bf16).T
        save(i).start()
        return carry

    lax.fori_loop(0, requests, body, 0)
    lax.fori_loop(0, requests, lambda i, c: (save(i).wait(), c)[1], 0)


def split(x, terms):
    out = []
    for _ in range(terms - 1):
        out.append(x.astype(bf16))
        x = x - out[-1].astype(f32)
    return out + [x.astype(bf16)]


def mix_kernel(
    arrive,
    recv_ref,
    wdt_ref,
    cxw_ref,
    cbw_ref,
    bias_ref,
    alog_ref,
    skip_ref,
    gain_ref,
    cvec_ref,
    cx_ref,
    cb_ref,
    wzx_hbm,
    wbc_hbm,
    wout_hbm,
    turned_hbm,
    out_hbm,
    push_hbm,
    b_hbm,
    dec_hbm,
    xin_hbm,
    bin_hbm,
    xw_ref,
    bw_ref,
    gate_ref,
    ec_ref,
    sc_ref,
    fd_ref,
    g_ref,
    sq_ref,
    out_ref,
    push_ref,
    b_ref,
    xin_ref,
    bin_ref,
    wzx_ref,
    wbc_ref,
    wout_ref,
    turned_ref,
    dec_ref,
    out_sem,
    side_sem,
    weight_sem,
    *,
    heads_dev,
):
    requests = cx_ref.shape[0]
    tail = cx_ref.shape[1]
    inner = xw_ref.shape[2]
    steps = recv_ref.shape[1]
    part = recv_ref.shape[2]
    peers = recv_ref.shape[0] // (2 * heads_dev)
    tokens = requests * steps
    nstate = b_ref.shape[2]
    heads = wdt_ref.shape[1]
    headdim = inner // heads
    spread = heads * steps
    base = 8 - tail
    blk = 256
    blocks = inner // blk

    load_zx, load_bc, load_turned, load_out = [
        pltpu.make_async_copy(src, dst, weight_sem.at[n])
        for n, (src, dst) in enumerate(
            [(wzx_hbm, wzx_ref), (wbc_hbm, wbc_ref), (turned_hbm, turned_ref), (wout_hbm, wout_ref)]
        )
    ]
    for copy in (load_zx, load_bc, load_turned, load_out):
        copy.start()

    def previous(i, carry):
        row = arrive[i]
        xw_ref[i, base:8, :] = cx_ref[row]
        bw_ref[i, base:8, :] = cb_ref[row]
        return carry

    lax.fori_loop(0, requests, previous, 0, unroll=4)

    view = recv_ref.reshape(peers, heads_dev, 2, steps, part)
    tok = jnp.concatenate(
        [view[:, h].reshape(tokens, part) for h in range(heads_dev)], axis=1
    )

    def proj(w):
        return jnp.dot(tok, w, preferred_element_type=f32).astype(bf16)

    dt_in = proj(wdt_ref[...]).astype(f32)
    load_zx.wait()
    load_bc.wait()
    for n in range(blocks):
        cols = slice(n * blk, (n + 1) * blk)
        x_n = proj(wzx_ref[:, inner + n * blk : inner + (n + 1) * blk])
        xin_ref[:, :, cols] = x_n.reshape(requests, steps, blk)
        xw_ref[:, 8 : 8 + steps, cols] = x_n.astype(f32).reshape(requests, steps, blk)
    bc_n = proj(wbc_ref[...])
    bin_ref[...] = bc_n.reshape(requests, steps, 2 * nstate)
    bw_ref[:, 8 : 8 + steps, :] = bc_n.astype(f32).reshape(requests, steps, 2 * nstate)
    side = [
        pltpu.make_async_copy(xin_ref, xin_hbm, side_sem.at[0]),
        pltpu.make_async_copy(bin_ref, bin_hbm, side_sem.at[1]),
        pltpu.make_async_copy(push_ref, push_hbm, side_sem.at[2]),
        pltpu.make_async_copy(b_ref, b_hbm, side_sem.at[3]),
        pltpu.make_async_copy(dec_ref, dec_hbm, side_sem.at[4]),
    ]
    side[0].start()
    side[1].start()
    for n in range(blocks):
        gate_ref[:, n * blk : (n + 1) * blk] = proj(wzx_ref[:, n * blk : (n + 1) * blk])

    pre = dt_in + bias_ref[...]
    dt = jnp.maximum(pre, 0.0) + jnp.log1p(jnp.exp(-jnp.abs(pre)))
    rate = -dt * jnp.exp(alog_ref[...])
    place = lax.rem(lax.broadcasted_iota(jnp.int32, (tokens, heads), 0), steps)
    cumul = rate
    d = 1
    while d < steps:
        cumul = cumul + jnp.where(place >= d, pltpu.roll(cumul, d, 0), 0.0)
        d *= 2
    live = place < cvec_ref[...]
    total = jnp.sum(jnp.where(live, rate, 0.0).reshape(requests, steps, heads), axis=1, keepdims=True)
    dec_ref[...] = jnp.exp(total)
    totals = jnp.broadcast_to(total, (requests, steps, heads)).reshape(tokens, heads)
    scaled = jnp.where(live, jnp.exp(jnp.where(live, totals - cumul, 0.0)) * dt, 0.0)

    def widen(x, width, each, terms):
        rows = lax.broadcasted_iota(jnp.int32, (heads, width), 0)
        cols = lax.div(lax.broadcasted_iota(jnp.int32, (heads, width), 1), each)
        pick = (rows == cols).astype(bf16)
        wide = None
        for term in split(x, terms):
            more = jnp.dot(term, pick, preferred_element_type=f32)
            wide = more if wide is None else wide + more
        return wide.reshape(requests, steps, width)

    ec_ref[...] = widen(jnp.exp(cumul), inner, headdim, 2)
    sc_ref[...] = widen(scaled, inner, headdim, 2)
    cum2 = widen(cumul, spread, steps, 3)
    dt2 = widen(dt, spread, steps, 2)
    t_at = lax.broadcasted_iota(jnp.int32, (1, steps, spread), 1)
    s_at = lax.rem(lax.broadcasted_iota(jnp.int32, (1, steps, spread), 2), steps)
    same = t_at == s_at
    lower = t_at >= s_at
    crow = jnp.sum(jnp.where(same, cum2, 0.0), axis=1, keepdims=True)
    drow = jnp.sum(jnp.where(same, dt2, 0.0), axis=1, keepdims=True)
    fd_ref[...] = jnp.where(lower, jnp.exp(jnp.where(lower, cum2 - crow, 0.0)) * drow, 0.0)

    group = heads // 2
    gspread, ginner = group * steps, group * headdim
    r_head = lax.div(lax.broadcasted_iota(jnp.int32, (gspread, ginner), 0), steps)
    c_head = lax.div(lax.broadcasted_iota(jnp.int32, (gspread, ginner), 1), headdim)
    diag = (r_head == c_head).astype(bf16)
    many = 8
    rows = many * steps
    own = lax.div(lax.broadcasted_iota(jnp.int32, (rows, rows), 0), steps) == lax.div(
        lax.broadcasted_iota(jnp.int32, (rows, rows), 1), steps
    )
    repeat = (
        lax.rem(lax.broadcasted_iota(jnp.int32, (rows, spread), 0), steps)
        == lax.rem(lax.broadcasted_iota(jnp.int32, (rows, spread), 1), steps)
    ).astype(bf16)

    def conv(win_ref, w_ref, at):
        total_c = w_ref[tail + 1 : tail + 2, :][None]
        for k in range(tail + 1):
            total_c = total_c + w_ref[k : k + 1, :][None] * win_ref[at, base + k : base + k + steps, :]
        return (total_c * lax.logistic(total_c)).astype(bf16)

    def body(n, carry):
        at = pl.ds(n * many, many)
        x = conv(xw_ref, cxw_ref, at)
        bc = conv(bw_ref, cbw_ref, at)
        b_ref[at] = bc[:, :, :nstate]
        b = bc[:, :, :nstate].reshape(rows, nstate)
        c = bc[:, :, nstate:].reshape(rows, nstate)
        gram = jnp.where(own, lax.dot_general(c, b, NT, preferred_element_type=f32), 0.0)
        spread_gram = sum(jnp.dot(t, repeat, preferred_element_type=f32) for t in split(gram, 2))
        factor = (spread_gram * fd_ref[at].reshape(rows, spread)).astype(bf16)
        parts = []
        for r in range(many):
            tok_r = slice(r * steps, (r + 1) * steps)
            carried = jnp.dot(c[tok_r], turned_ref[n * many + r], preferred_element_type=f32)
            within = jnp.concatenate(
                [
                    jnp.dot(
                        factor[tok_r, g * gspread : (g + 1) * gspread],
                        jnp.concatenate([x[r, :, g * ginner : (g + 1) * ginner]] * group, axis=0)
                        * diag,
                        preferred_element_type=f32,
                    )
                    for g in range(2)
                ],
                axis=1,
            )
            parts.append(carried * ec_ref[n * many + r] + within)
        xf = x.astype(f32).reshape(rows, inner)
        mixed = (jnp.concatenate(parts, axis=0) + skip_ref[...] * xf).astype(bf16)
        push_ref[at] = (xf * sc_ref[at].reshape(rows, inner)).astype(bf16).reshape(many, steps, inner)
        tok_at = pl.ds(pl.multiple_of(n * rows, rows), rows)
        gate = gate_ref[tok_at, :].astype(f32)
        gated = mixed.astype(f32) * (gate * lax.logistic(gate))
        sq_ref[tok_at, :] = (gated * gated).astype(bf16)
        g_ref[tok_at, :] = (gated * gain_ref[...]).astype(bf16)
        return carry

    load_turned.wait()
    load_out.wait()
    lax.fori_loop(0, requests // many, body, 0)

    side[2].start()
    side[3].start()
    side[4].start()

    ones = jnp.ones((STAT_ROWS, inner), bf16)
    squares = lax.dot_general(ones, sq_ref[...], NT, preferred_element_type=f32)
    high = squares.astype(bf16).astype(f32)
    first = lax.broadcasted_iota(jnp.int32, squares.shape, 0) == 0
    stats = jnp.where(first, high, squares - high).astype(bf16)
    pair = 2 * steps
    data_rows = 2 * pair

    def leave(h):
        return pltpu.make_async_copy(out_ref.at[:, h], out_hbm.at[:, h], out_sem.at[h])

    for b in range(peers):
        piece = jnp.concatenate(
            [stats[:, b * pair : (b + 1) * pair], jnp.zeros((STAT_ROWS, 128 - pair), bf16)], axis=1
        )
        for h in range(heads_dev):
            out_ref[b, h, data_rows:, :] = piece

    for h in range(heads_dev):
        res = jnp.dot(
            g_ref[...], wout_ref[:, h * part : (h + 1) * part], preferred_element_type=f32
        ).astype(bf16)
        out_ref[:, h, 0:pair, :] = res[:, :128].reshape(peers, pair, 128)
        out_ref[:, h, pair:data_rows, :] = res[:, 128:].reshape(peers, pair, 128)
        leave(h).start()
    for h in range(heads_dev):
        leave(h).wait()
    for copy in side:
        copy.wait()


def state_kernel(
    arrive,
    push_ref,
    b_ref,
    dec_ref,
    xin_ref,
    bin_ref,
    cx_ref,
    cb_ref,
    state_hbm,
    newstate_hbm,
    ncx_ref,
    ncb_ref,
    xw_ref,
    bw_ref,
    st_ref,
    in_sem,
    out_sem,
):
    requests, steps, inner = push_ref.shape
    tail = ncx_ref.shape[1]
    nstate = b_ref.shape[2]
    heads = dec_ref.shape[2]
    headdim = inner // heads
    base = 8 - tail

    def load_state(i):
        return pltpu.make_async_copy(state_hbm.at[arrive[i]], st_ref.at[i], in_sem.at[i])

    def save_state(i):
        return pltpu.make_async_copy(st_ref.at[i], newstate_hbm.at[arrive[i]], out_sem.at[i])

    lax.fori_loop(0, requests, lambda i, c: (load_state(i).start(), c)[1], 0)

    def body(i, carry):
        row = arrive[i]
        back = steps + tail - arrive[requests + i]
        xw_ref[i, base:8, :] = cx_ref[row]
        xw_ref[i, 8:, :] = xin_ref[i].astype(f32)
        bw_ref[i, base:8, :] = cb_ref[row]
        bw_ref[i, 8:, :] = bin_ref[i].astype(f32)
        ncx_ref[row] = pltpu.roll(xw_ref[i], back, 0)[:tail]
        ncb_ref[row] = pltpu.roll(bw_ref[i], back, 0)[:tail]
        update = lax.dot_general(push_ref[i], b_ref[i], TN, preferred_element_type=f32)
        dec = dec_ref[i]
        load_state(i).wait()
        for h in range(heads):
            sl = slice(h * headdim, (h + 1) * headdim)
            factor_h = jnp.broadcast_to(dec[:, h : h + 1], (headdim, nstate))
            st_ref[i, sl, :] = factor_h * st_ref[i, sl, :] + update[sl, :]
        save_state(i).start()
        return carry

    lax.fori_loop(0, requests, body, 0)
    lax.fori_loop(0, requests, lambda i, c: (save_state(i).wait(), c)[1], 0)


def final_kernel(slot_ref, len_ref, recv_ref, out_ref, seen, *, heads_dev, inner_all):
    requests, steps, part = out_ref.shape
    peers = seen.shape[0]
    pair = 2 * steps
    data_rows = 2 * pair
    base = lax.axis_index("req") * requests
    for o in range(peers):
        seen[o] = 0
    view = recv_ref.reshape(peers, heads_dev, data_rows + STAT_ROWS, 128)
    place = lax.broadcasted_iota(jnp.int32, (steps, 128), 0)
    lane = lax.broadcasted_iota(jnp.int32, (steps, 128), 1)

    def body(i, carry):
        owner = lax.div(slot_ref[base + i], requests)
        length = len_ref[base + i]
        j = seen[owner]
        seen[owner] = j + 1
        stats = view[owner, 0, data_rows:, :].astype(f32)
        for h in range(1, heads_dev):
            stats = stats + view[owner, h, data_rows:, :].astype(f32)
        squares = stats[0:1, :] + stats[1:2, :]
        total = jnp.sum(jnp.where(lane == place + j * steps, squares, 0.0), axis=1, keepdims=True)
        scale = jnp.where(place < length, lax.rsqrt(total / inner_all + 1e-05), 0.0)
        for half in range(2):
            rows = pl.ds(pl.multiple_of(half * pair + j * steps, steps), steps)
            acc = view[owner, 0, rows, :].astype(f32)
            for h in range(1, heads_dev):
                acc = acc + view[owner, h, rows, :].astype(f32)
            out_ref[i, :, half * 128 : (half + 1) * 128] = jnp.where(
                place < length, acc * scale, 0.0
            ).astype(bf16)
        return carry

    lax.fori_loop(0, requests, body, 0, unroll=4)


def vmem(n):
    return [pl.BlockSpec(memory_space=pltpu.VMEM)] * n


def smem():
    return pl.BlockSpec(memory_space=pltpu.SMEM)


def hbm(n):
    return [pl.BlockSpec(memory_space=pltpu.HBM)] * n


def in_hbm(x):
    return pltpu.with_memory_space_constraint(x, pltpu.HBM)


def per_device(
    hidden,
    w_zx,
    w_bc,
    w_dt,
    conv_x_w,
    conv_bc_w,
    dt_bias,
    a_log,
    d_skip,
    norm_gain,
    w_out,
    ssm_state,
    conv_x_state,
    conv_bc_state,
    slot,
    lengths,
    accepted,
):
    requests, steps, part = hidden.shape
    width = w_zx.shape[0]
    inner = w_zx.shape[2]
    bc_cols = w_bc.shape[1]
    heads = w_dt.shape[1]
    headdim = inner // heads
    nstate = bc_cols // 2
    tail = conv_x_state.shape[1]
    peers = lax.axis_size("req")
    heads_dev = lax.axis_size("head")
    tokens = requests * steps
    spread = heads * steps
    out_rows = 4 * steps + STAT_ROWS
    me = lax.axis_index("req")

    slot_blocks = slot.reshape(peers, requests)
    outgoing = pl.pallas_call(
        functools.partial(send_kernel, heads_dev=heads_dev),
        out_shape=pltpu.HBM((peers * heads_dev * 2, steps, part), bf16),
        in_specs=[smem()] + vmem(1),
        out_specs=hbm(1)[0],
        scratch_shapes=[
            pltpu.VMEM((peers * heads_dev * 2, steps, part), bf16),
            pltpu.SMEM((peers,), jnp.int32),
            pltpu.SMEM((requests,), jnp.int32),
            pltpu.SemaphoreType.DMA((peers,)),
        ],
        compiler_params=pltpu.CompilerParams(vmem_limit_bytes=4 * MIB),
        name="send_rows",
    )(in_hbm(slot), in_hbm(hidden))
    arrived = lax.all_to_all(outgoing, ("req", "head"), split_axis=0, concat_axis=0, tiled=True)

    counted = jnp.minimum(accepted, lengths).reshape(peers, requests)
    order = jnp.arange(requests, dtype=jnp.int32)[None, :]
    code = (order * requests + slot_blocks % requests) * (2 * steps) + counted
    here = slot_blocks // requests == me
    low = jnp.min(jnp.where(here, code, jnp.iinfo(jnp.int32).max), axis=1)
    high = jnp.max(jnp.where(here, code, -1), axis=1)
    both = jnp.stack([low, high], axis=1).reshape(requests)
    rows = (both // (2 * steps)) % requests
    counts = both % (2 * steps)
    arrive = jnp.concatenate([rows, counts])
    count_col = jnp.broadcast_to(counts[:, None, None], (requests, steps, heads)).reshape(tokens, heads)

    states = in_hbm(ssm_state.reshape(requests, inner, nstate))
    turned = pl.pallas_call(
        stage_kernel,
        out_shape=pltpu.HBM((requests, nstate, inner), bf16),
        in_specs=[smem()] + hbm(1),
        out_specs=hbm(1)[0],
        scratch_shapes=[
            pltpu.VMEM((requests, inner, nstate), f32),
            pltpu.VMEM((requests, nstate, inner), bf16),
            pltpu.SemaphoreType.DMA((requests,)),
            pltpu.SemaphoreType.DMA((requests,)),
        ],
        compiler_params=pltpu.CompilerParams(vmem_limit_bytes=STAGE_MIB * MIB),
        cost_estimate=pl.CostEstimate(flops=10**9, bytes_accessed=20 * MIB, transcendentals=0),
        name="stage",
    )(arrive, states)
    leaving, push, b_conv, decay, x_in, bc_in = pl.pallas_call(
        functools.partial(mix_kernel, heads_dev=heads_dev),
        out_shape=(
            pltpu.HBM((peers, heads_dev, out_rows, 128), bf16),
            pltpu.HBM((requests, steps, inner), bf16),
            pltpu.HBM((requests, steps, nstate), bf16),
            pltpu.HBM((requests, 1, heads), f32),
            pltpu.HBM((requests, steps, inner), bf16),
            pltpu.HBM((requests, steps, bc_cols), bf16),
        ),
        in_specs=[smem()] + vmem(11) + hbm(4),
        out_specs=tuple(hbm(6)),
        scratch_shapes=[
            pltpu.VMEM((requests, 8 + steps, inner), f32),
            pltpu.VMEM((requests, 8 + steps, bc_cols), f32),
            pltpu.VMEM((tokens, inner), bf16),
            pltpu.VMEM((requests, steps, inner), f32),
            pltpu.VMEM((requests, steps, inner), f32),
            pltpu.VMEM((requests, steps, spread), f32),
            pltpu.VMEM((tokens, inner), bf16),
            pltpu.VMEM((tokens, inner), bf16),
            pltpu.VMEM((peers, heads_dev, out_rows, 128), bf16),
            pltpu.VMEM((requests, steps, inner), bf16),
            pltpu.VMEM((requests, steps, nstate), bf16),
            pltpu.VMEM((requests, steps, inner), bf16),
            pltpu.VMEM((requests, steps, bc_cols), bf16),
            pltpu.VMEM((width, 2 * inner), bf16),
            pltpu.VMEM((width, bc_cols), bf16),
            pltpu.VMEM((inner, width), bf16),
            pltpu.VMEM((requests, nstate, inner), bf16),
            pltpu.VMEM((requests, 1, heads), f32),
            pltpu.SemaphoreType.DMA((heads_dev,)),
            pltpu.SemaphoreType.DMA((5,)),
            pltpu.SemaphoreType.DMA((4,)),
        ],
        compiler_params=pltpu.CompilerParams(vmem_limit_bytes=MIX_MIB * MIB),
        cost_estimate=pl.CostEstimate(flops=4 * 10**9, bytes_accessed=8 * MIB, transcendentals=10**6),
        name="mix",
    )(
        arrive,
        arrived,
        w_dt,
        conv_x_w,
        conv_bc_w,
        dt_bias[None, :],
        a_log[None, :],
        jnp.repeat(d_skip, headdim)[None, :],
        norm_gain[None, :],
        count_col,
        conv_x_state,
        conv_bc_state,
        in_hbm(w_zx.reshape(width, 2 * inner)),
        in_hbm(w_bc),
        in_hbm(w_out),
        in_hbm(turned),
    )
    leaving = leaving.reshape(peers * heads_dev, out_rows, 128)
    returned = lax.all_to_all(leaving, ("req", "head"), split_axis=0, concat_axis=0, tiled=True)
    new_state, new_conv_x, new_conv_bc = pl.pallas_call(
        state_kernel,
        out_shape=(
            pltpu.HBM((requests, inner, nstate), f32),
            jax.ShapeDtypeStruct(conv_x_state.shape, f32),
            jax.ShapeDtypeStruct(conv_bc_state.shape, f32),
        ),
        in_specs=[smem()] + vmem(7) + hbm(1),
        out_specs=tuple(hbm(1) + vmem(2)),
        scratch_shapes=[
            pltpu.VMEM((requests, 8 + steps, inner), f32),
            pltpu.VMEM((requests, 8 + steps, bc_cols), f32),
            pltpu.VMEM((requests, inner, nstate), f32),
            pltpu.SemaphoreType.DMA((requests,)),
            pltpu.SemaphoreType.DMA((requests,)),
        ],
        compiler_params=pltpu.CompilerParams(vmem_limit_bytes=STATE_MIB * MIB),
        cost_estimate=pl.CostEstimate(flops=2 * 10**9, bytes_accessed=20 * MIB, transcendentals=0),
        name="update",
    )(arrive, push, b_conv, decay, x_in, bc_in, conv_x_state, conv_bc_state, states)
    out = pl.pallas_call(
        functools.partial(final_kernel, heads_dev=heads_dev, inner_all=inner * heads_dev),
        out_shape=jax.ShapeDtypeStruct((requests, steps, part), bf16),
        in_specs=[smem(), smem()] + vmem(1),
        out_specs=vmem(1)[0],
        scratch_shapes=[pltpu.SMEM((peers,), jnp.int32)],
        compiler_params=pltpu.CompilerParams(vmem_limit_bytes=4 * MIB),
        name="place_rows",
    )(slot, lengths, returned)
    return (out, new_state.reshape(ssm_state.shape), new_conv_x, new_conv_bc)


def solution(mesh):
    in_specs = (
        P("req", None, "head"),
        P(None, None, "head"),
        P(),
        P(None, "head"),
        P(None, "head"),
        P(),
        P("head"),
        P("head"),
        P("head"),
        P("head"),
        P("head", None),
        P("req", "head", None, None),
        P("req", None, "head"),
        P("req", None, None),
        P(),
        P(),
        P(),
    )
    out_specs = (
        P("req", None, "head"),
        P("req", "head", None, None),
        P("req", None, "head"),
        P("req", None, None),
    )
    return jax.shard_map(
        per_device, mesh=mesh, in_specs=in_specs, out_specs=out_specs, check_vma=False
    )
```

```python
import functools

import jax
import jax.numpy as jnp
from jax import lax
from jax.experimental import pallas as pl
from jax.experimental.pallas import tpu as pltpu
from jax.sharding import PartitionSpec as P

f32 = jnp.float32
bf16 = jnp.bfloat16
NT = (((1,), (1,)), ((), ()))
TN = (((0,), (0,)), ((), ()))
STAT_ROWS = 4
MIB = 1024 * 1024
MIX_MIB = 36
STAGE_MIB = 14
STATE_MIB = 16


def visit(slot_ref, first, requests, act):
    def body(i, met):
        owner = lax.div(slot_ref[first + i], requests)
        bit = lax.shift_left(jnp.int32(1), owner)
        act(i, owner, lax.min(met & bit, 1))
        return met | bit

    lax.fori_loop(0, requests, body, jnp.int32(0), unroll=8)


def send_kernel(slot_ref, hid_ref, out_hbm, buf, sem, *, heads_dev):
    requests = hid_ref.shape[0]
    peers = buf.shape[0] // (2 * heads_dev)

    def block(o):
        at = pl.ds(o * 2 * heads_dev, 2 * heads_dev)
        return pltpu.make_async_copy(buf.at[at], out_hbm.at[at], sem.at[o])

    def place(i, owner, j):
        rows = hid_ref[i]
        for h in range(heads_dev):
            buf[(owner * heads_dev + h) * 2 + j] = rows

        @pl.when(j == 1)
        def _():
            block(owner).start()

    visit(slot_ref, lax.axis_index("req") * requests, requests, place)
    lax.fori_loop(0, peers, lambda o, c: (block(o).wait(), c)[1], 0)


def stage_kernel(arrive, state_hbm, turned_hbm, st_ref, turned_ref, in_sem, out_sem):
    requests = turned_ref.shape[0]

    def load_state(i):
        return pltpu.make_async_copy(state_hbm.at[arrive[i]], st_ref.at[i], in_sem.at[i])

    def save(i):
        return pltpu.make_async_copy(turned_ref.at[i], turned_hbm.at[i], out_sem.at[i])

    lax.fori_loop(0, requests, lambda i, c: (load_state(i).start(), c)[1], 0)

    def body(i, carry):
        load_state(i).wait()
        turned_ref[i] = st_ref[i].astype(bf16).T
        save(i).start()
        return carry

    lax.fori_loop(0, requests, body, 0)
    lax.fori_loop(0, requests, lambda i, c: (save(i).wait(), c)[1], 0)


def split(x, terms):
    out = []
    for _ in range(terms - 1):
        out.append(x.astype(bf16))
        x = x - out[-1].astype(f32)
    return out + [x.astype(bf16)]


def mix_kernel(
    arrive,
    recv_ref,
    wdt_ref,
    cxw_ref,
    cbw_ref,
    bias_ref,
    alog_ref,
    skip_ref,
    gain_ref,
    cvec_ref,
    cx_ref,
    cb_ref,
    wzx_hbm,
    wbc_hbm,
    wout_hbm,
    turned_hbm,
    out_hbm,
    push_hbm,
    b_hbm,
    dec_hbm,
    xin_hbm,
    bin_hbm,
    xw_ref,
    bw_ref,
    gate_ref,
    ec_ref,
    sc_ref,
    fd_ref,
    g_ref,
    sq_ref,
    out_ref,
    push_ref,
    b_ref,
    xin_ref,
    bin_ref,
    wzx_ref,
    wbc_ref,
    wout_ref,
    turned_ref,
    dec_ref,
    out_sem,
    side_sem,
    weight_sem,
    *,
    heads_dev,
):
    requests = cx_ref.shape[0]
    tail = cx_ref.shape[1]
    inner = xw_ref.shape[2]
    steps = recv_ref.shape[1]
    part = recv_ref.shape[2]
    peers = recv_ref.shape[0] // (2 * heads_dev)
    tokens = requests * steps
    nstate = b_ref.shape[2]
    heads = wdt_ref.shape[1]
    headdim = inner // heads
    spread = heads * steps
    base = 8 - tail
    blk = 256
    blocks = inner // blk

    z_cols, x_cols = pl.ds(0, inner), pl.ds(inner, inner)
    load_x, load_bc, load_z, load_turned, load_out = [
        pltpu.make_async_copy(src, dst, weight_sem.at[n])
        for n, (src, dst) in enumerate(
            [
                (wzx_hbm.at[:, x_cols], wzx_ref.at[:, x_cols]),
                (wbc_hbm, wbc_ref),
                (wzx_hbm.at[:, z_cols], wzx_ref.at[:, z_cols]),
                (turned_hbm, turned_ref),
                (wout_hbm, wout_ref),
            ]
        )
    ]
    for copy in (load_x, load_bc, load_z, load_turned, load_out):
        copy.start()

    def previous(i, carry):
        row = arrive[i]
        xw_ref[i, base:8, :] = cx_ref[row]
        bw_ref[i, base:8, :] = cb_ref[row]
        return carry

    lax.fori_loop(0, requests, previous, 0, unroll=4)

    view = recv_ref.reshape(peers, heads_dev, 2, steps, part)
    tok = jnp.concatenate(
        [view[:, h].reshape(tokens, part) for h in range(heads_dev)], axis=1
    )

    def proj(w):
        return jnp.dot(tok, w, preferred_element_type=f32).astype(bf16)

    dt_in = proj(wdt_ref[...]).astype(f32)
    load_x.wait()
    load_bc.wait()
    for n in range(blocks):
        cols = slice(n * blk, (n + 1) * blk)
        x_n = proj(wzx_ref[:, inner + n * blk : inner + (n + 1) * blk])
        xin_ref[:, :, cols] = x_n.reshape(requests, steps, blk)
        xw_ref[:, 8 : 8 + steps, cols] = x_n.astype(f32).reshape(requests, steps, blk)
    bc_n = proj(wbc_ref[...])
    bin_ref[...] = bc_n.reshape(requests, steps, 2 * nstate)
    bw_ref[:, 8 : 8 + steps, :] = bc_n.astype(f32).reshape(requests, steps, 2 * nstate)
    side = [
        pltpu.make_async_copy(xin_ref, xin_hbm, side_sem.at[0]),
        pltpu.make_async_copy(bin_ref, bin_hbm, side_sem.at[1]),
        pltpu.make_async_copy(push_ref, push_hbm, side_sem.at[2]),
        pltpu.make_async_copy(b_ref, b_hbm, side_sem.at[3]),
        pltpu.make_async_copy(dec_ref, dec_hbm, side_sem.at[4]),
    ]
    side[0].start()
    side[1].start()
    load_z.wait()
    for n in range(blocks):
        gate_ref[:, n * blk : (n + 1) * blk] = proj(wzx_ref[:, n * blk : (n + 1) * blk])

    pre = dt_in + bias_ref[...]
    dt = jnp.maximum(pre, 0.0) + jnp.log1p(jnp.exp(-jnp.abs(pre)))
    rate = -dt * jnp.exp(alog_ref[...])
    place = lax.rem(lax.broadcasted_iota(jnp.int32, (tokens, heads), 0), steps)
    cumul = rate
    d = 1
    while d < steps:
        cumul = cumul + jnp.where(place >= d, pltpu.roll(cumul, d, 0), 0.0)
        d *= 2
    live = place < cvec_ref[...]
    total = jnp.sum(jnp.where(live, rate, 0.0).reshape(requests, steps, heads), axis=1, keepdims=True)
    dec_ref[...] = jnp.exp(total)
    totals = jnp.broadcast_to(total, (requests, steps, heads)).reshape(tokens, heads)
    scaled = jnp.where(live, jnp.exp(jnp.where(live, totals - cumul, 0.0)) * dt, 0.0)

    def widen(x, width, each, terms):
        rows = lax.broadcasted_iota(jnp.int32, (heads, width), 0)
        cols = lax.div(lax.broadcasted_iota(jnp.int32, (heads, width), 1), each)
        pick = (rows == cols).astype(bf16)
        wide = None
        for term in split(x, terms):
            more = jnp.dot(term, pick, preferred_element_type=f32)
            wide = more if wide is None else wide + more
        return wide.reshape(requests, steps, width)

    ec_ref[...] = widen(jnp.exp(cumul), inner, headdim, 2)
    sc_ref[...] = widen(scaled, inner, headdim, 2)
    cum2 = widen(cumul, spread, steps, 3)
    dt2 = widen(dt, spread, steps, 2)
    t_at = lax.broadcasted_iota(jnp.int32, (1, steps, spread), 1)
    s_at = lax.rem(lax.broadcasted_iota(jnp.int32, (1, steps, spread), 2), steps)
    same = t_at == s_at
    lower = t_at >= s_at
    crow = jnp.sum(jnp.where(same, cum2, 0.0), axis=1, keepdims=True)
    drow = jnp.sum(jnp.where(same, dt2, 0.0), axis=1, keepdims=True)
    fd_ref[...] = jnp.where(lower, jnp.exp(jnp.where(lower, cum2 - crow, 0.0)) * drow, 0.0)

    group = heads // 2
    gspread, ginner = group * steps, group * headdim
    r_head = lax.div(lax.broadcasted_iota(jnp.int32, (gspread, ginner), 0), steps)
    c_head = lax.div(lax.broadcasted_iota(jnp.int32, (gspread, ginner), 1), headdim)
    diag = (r_head == c_head).astype(bf16)
    many = 8
    rows = many * steps
    own = lax.div(lax.broadcasted_iota(jnp.int32, (rows, rows), 0), steps) == lax.div(
        lax.broadcasted_iota(jnp.int32, (rows, rows), 1), steps
    )
    repeat = (
        lax.rem(lax.broadcasted_iota(jnp.int32, (rows, spread), 0), steps)
        == lax.rem(lax.broadcasted_iota(jnp.int32, (rows, spread), 1), steps)
    ).astype(bf16)

    def conv(win_ref, w_ref, at):
        total_c = w_ref[tail + 1 : tail + 2, :][None]
        for k in range(tail + 1):
            total_c = total_c + w_ref[k : k + 1, :][None] * win_ref[at, base + k : base + k + steps, :]
        return (total_c * lax.logistic(total_c)).astype(bf16)

    def body(n):
        at = slice(n * many, (n + 1) * many)
        x = conv(xw_ref, cxw_ref, at)
        bc = conv(bw_ref, cbw_ref, at)
        b_ref[at] = bc[:, :, :nstate]
        b = bc[:, :, :nstate].reshape(rows, nstate)
        c = bc[:, :, nstate:].reshape(rows, nstate)
        gram = jnp.where(own, lax.dot_general(c, b, NT, preferred_element_type=f32), 0.0)
        spread_gram = sum(jnp.dot(t, repeat, preferred_element_type=f32) for t in split(gram, 2))
        factor = (spread_gram * fd_ref[at].reshape(rows, spread)).astype(bf16)
        parts = []
        for r in range(many):
            tok_r = slice(r * steps, (r + 1) * steps)
            carried = jnp.dot(c[tok_r], turned_ref[n * many + r], preferred_element_type=f32)
            within = jnp.concatenate(
                [
                    jnp.dot(
                        factor[tok_r, g * gspread : (g + 1) * gspread],
                        jnp.concatenate([x[r, :, g * ginner : (g + 1) * ginner]] * group, axis=0)
                        * diag,
                        preferred_element_type=f32,
                    )
                    for g in range(2)
                ],
                axis=1,
            )
            parts.append(carried * ec_ref[n * many + r] + within)
        xf = x.astype(f32).reshape(rows, inner)
        mixed = (jnp.concatenate(parts, axis=0) + skip_ref[...] * xf).astype(bf16)
        push_ref[at] = (xf * sc_ref[at].reshape(rows, inner)).astype(bf16).reshape(many, steps, inner)
        tok_at = slice(n * rows, (n + 1) * rows)
        gate = gate_ref[tok_at, :].astype(f32)
        gated = mixed.astype(f32) * (gate * lax.logistic(gate))
        sq_ref[tok_at, :] = (gated * gated).astype(bf16)
        g_ref[tok_at, :] = (gated * gain_ref[...]).astype(bf16)

    load_turned.wait()
    load_out.wait()
    for n in range(requests // many):
        body(n)

    side[2].start()
    side[3].start()
    side[4].start()

    ones = jnp.ones((8, inner), bf16)
    squares = lax.dot_general(ones, sq_ref[...], NT, preferred_element_type=f32)
    high = squares.astype(bf16).astype(f32)
    first = lax.broadcasted_iota(jnp.int32, squares.shape, 0) == 0
    stats = jnp.where(first, high, squares - high).astype(bf16)
    pair = 2 * steps
    data_rows = 2 * pair

    def leave(h):
        return pltpu.make_async_copy(out_ref.at[:, h], out_hbm.at[:, h], out_sem.at[h])

    for b in range(peers):
        piece = jnp.concatenate(
            [stats[:STAT_ROWS, b * pair : (b + 1) * pair], jnp.zeros((STAT_ROWS, 128 - pair), bf16)], axis=1
        )
        for h in range(heads_dev):
            out_ref[b, h, data_rows // STAT_ROWS] = piece

    for h in range(heads_dev):
        res = jnp.dot(
            g_ref[...], wout_ref[:, h * part : (h + 1) * part], preferred_element_type=f32
        ).astype(bf16)
        part_rows = pair // STAT_ROWS
        out_ref[:, h, :part_rows] = res[:, :128].reshape(peers, part_rows, STAT_ROWS, 128)
        out_ref[:, h, part_rows : 2 * part_rows] = res[:, 128:].reshape(peers, part_rows, STAT_ROWS, 128)
        leave(h).start()
    for h in range(heads_dev):
        leave(h).wait()
    for copy in side:
        copy.wait()


def state_kernel(
    arrive,
    push_ref,
    b_ref,
    dec_ref,
    xin_ref,
    bin_ref,
    cx_ref,
    cb_ref,
    state_hbm,
    newstate_hbm,
    ncx_ref,
    ncb_ref,
    xw_ref,
    bw_ref,
    st_ref,
    in_sem,
    out_sem,
):
    requests, steps, inner = push_ref.shape
    tail = ncx_ref.shape[1]
    nstate = b_ref.shape[2]
    heads = dec_ref.shape[2]
    headdim = inner // heads
    base = 8 - tail

    def load_state(i):
        return pltpu.make_async_copy(state_hbm.at[arrive[i]], st_ref.at[i], in_sem.at[i])

    def save_state(i):
        return pltpu.make_async_copy(st_ref.at[i], newstate_hbm.at[arrive[i]], out_sem.at[i])

    lax.fori_loop(0, requests, lambda i, c: (load_state(i).start(), c)[1], 0)

    def body(i, carry):
        row = arrive[i]
        back = steps + tail - arrive[requests + i]
        xw_ref[i, base:8, :] = cx_ref[row]
        xw_ref[i, 8:, :] = xin_ref[i].astype(f32)
        bw_ref[i, base:8, :] = cb_ref[row]
        bw_ref[i, 8:, :] = bin_ref[i].astype(f32)
        ncx_ref[row] = pltpu.roll(xw_ref[i], back, 0)[:tail]
        ncb_ref[row] = pltpu.roll(bw_ref[i], back, 0)[:tail]
        update = lax.dot_general(push_ref[i], b_ref[i], TN, preferred_element_type=f32)
        dec = dec_ref[i]
        load_state(i).wait()
        for h in range(heads):
            sl = slice(h * headdim, (h + 1) * headdim)
            factor_h = jnp.broadcast_to(dec[:, h : h + 1], (headdim, nstate))
            st_ref[i, sl, :] = factor_h * st_ref[i, sl, :] + update[sl, :]
        save_state(i).start()
        return carry

    lax.fori_loop(0, requests, body, 0)
    lax.fori_loop(0, requests, lambda i, c: (save_state(i).wait(), c)[1], 0)


def final_kernel(slot_ref, len_ref, recv_ref, out_ref, order, *, heads_dev, inner_all):
    requests, steps, part = out_ref.shape
    peers = requests // 2
    pair = 2 * steps
    data_rows = 2 * pair
    base = lax.axis_index("req") * requests

    def note(i, owner, j):
        order[owner * 2 + j] = i

    visit(slot_ref, base, requests, note)
    groups = data_rows // STAT_ROWS
    view = recv_ref.reshape(peers, heads_dev, groups + 1, STAT_ROWS, 128)
    own = lax.broadcasted_iota(jnp.int32, (pair, 128), 0) == lax.broadcasted_iota(
        jnp.int32, (pair, 128), 1
    )
    place = lax.broadcasted_iota(jnp.int32, (steps, 128), 0)

    def body(o, carry):
        stats = view[o, 0, groups].astype(f32)
        acc = view[o, 0, :groups].astype(f32)
        for h in range(1, heads_dev):
            stats = stats + view[o, h, groups].astype(f32)
            acc = acc + view[o, h, :groups].astype(f32)
        acc = acc.reshape(data_rows, 128)
        squares = stats[0:1, :] + stats[1:2, :]
        total = jnp.sum(jnp.where(own, squares, 0.0), axis=1, keepdims=True)
        scale = lax.rsqrt(total / inner_all + 1e-05)
        for j in range(2):
            i = order[o * 2 + j]
            keep = place < len_ref[base + i]
            for half in range(2):
                at = half * pair + j * steps
                value = acc[at : at + steps, :] * scale[j * steps : (j + 1) * steps, :]
                out_ref[i, :, half * 128 : (half + 1) * 128] = jnp.where(keep, value, 0.0).astype(bf16)
        return carry

    lax.fori_loop(0, peers, body, 0, unroll=4)


def vmem(n):
    return [pl.BlockSpec(memory_space=pltpu.VMEM)] * n


def smem():
    return pl.BlockSpec(memory_space=pltpu.SMEM)


def hbm(n):
    return [pl.BlockSpec(memory_space=pltpu.HBM)] * n


def in_hbm(x):
    return pltpu.with_memory_space_constraint(x, pltpu.HBM)


def per_device(
    hidden,
    w_zx,
    w_bc,
    w_dt,
    conv_x_w,
    conv_bc_w,
    dt_bias,
    a_log,
    d_skip,
    norm_gain,
    w_out,
    ssm_state,
    conv_x_state,
    conv_bc_state,
    slot,
    lengths,
    accepted,
):
    requests, steps, part = hidden.shape
    width = w_zx.shape[0]
    inner = w_zx.shape[2]
    bc_cols = w_bc.shape[1]
    heads = w_dt.shape[1]
    headdim = inner // heads
    nstate = bc_cols // 2
    tail = conv_x_state.shape[1]
    peers = lax.axis_size("req")
    heads_dev = lax.axis_size("head")
    tokens = requests * steps
    spread = heads * steps
    out_rows = 4 * steps // STAT_ROWS + 1
    me = lax.axis_index("req")

    slot_blocks = slot.reshape(peers, requests)
    outgoing = pl.pallas_call(
        functools.partial(send_kernel, heads_dev=heads_dev),
        out_shape=pltpu.HBM((peers * heads_dev * 2, steps, part), bf16),
        in_specs=[smem()] + vmem(1),
        out_specs=hbm(1)[0],
        scratch_shapes=[
            pltpu.VMEM((peers * heads_dev * 2, steps, part), bf16),
            pltpu.SemaphoreType.DMA((peers,)),
        ],
        compiler_params=pltpu.CompilerParams(vmem_limit_bytes=4 * MIB),
        name="send_rows",
    )(in_hbm(slot), in_hbm(hidden))
    arrived = lax.all_to_all(outgoing, ("req", "head"), split_axis=0, concat_axis=0, tiled=True)

    counted = jnp.minimum(accepted, lengths).reshape(peers, requests)
    order = jnp.arange(requests, dtype=jnp.int32)[None, :]
    code = (order * requests + slot_blocks % requests) * (2 * steps) + counted
    here = slot_blocks // requests == me
    low = jnp.min(jnp.where(here, code, jnp.iinfo(jnp.int32).max), axis=1)
    high = jnp.max(jnp.where(here, code, -1), axis=1)
    both = jnp.stack([low, high], axis=1).reshape(requests)
    rows = (both // (2 * steps)) % requests
    counts = both % (2 * steps)
    arrive = jnp.concatenate([rows, counts])
    count_col = jnp.broadcast_to(counts[:, None, None], (requests, steps, heads)).reshape(tokens, heads)

    states = in_hbm(ssm_state.reshape(requests, inner, nstate))
    turned = pl.pallas_call(
        stage_kernel,
        out_shape=pltpu.HBM((requests, nstate, inner), bf16),
        in_specs=[smem()] + hbm(1),
        out_specs=hbm(1)[0],
        scratch_shapes=[
            pltpu.VMEM((requests, inner, nstate), f32),
            pltpu.VMEM((requests, nstate, inner), bf16),
            pltpu.SemaphoreType.DMA((requests,)),
            pltpu.SemaphoreType.DMA((requests,)),
        ],
        compiler_params=pltpu.CompilerParams(vmem_limit_bytes=STAGE_MIB * MIB),
        cost_estimate=pl.CostEstimate(flops=10**9, bytes_accessed=20 * MIB, transcendentals=0),
        name="stage",
    )(arrive, states)
    leaving, push, b_conv, decay, x_in, bc_in = pl.pallas_call(
        functools.partial(mix_kernel, heads_dev=heads_dev),
        out_shape=(
            pltpu.HBM((peers, heads_dev, out_rows, STAT_ROWS, 128), bf16),
            pltpu.HBM((requests, steps, inner), bf16),
            pltpu.HBM((requests, steps, nstate), bf16),
            pltpu.HBM((requests, 1, heads), f32),
            pltpu.HBM((requests, steps, inner), bf16),
            pltpu.HBM((requests, steps, bc_cols), bf16),
        ),
        in_specs=[smem()] + vmem(11) + hbm(4),
        out_specs=tuple(hbm(6)),
        scratch_shapes=[
            pltpu.VMEM((requests, 8 + steps, inner), f32),
            pltpu.VMEM((requests, 8 + steps, bc_cols), f32),
            pltpu.VMEM((tokens, inner), bf16),
            pltpu.VMEM((requests, steps, inner), f32),
            pltpu.VMEM((requests, steps, inner), f32),
            pltpu.VMEM((requests, steps, spread), f32),
            pltpu.VMEM((tokens, inner), bf16),
            pltpu.VMEM((tokens, inner), bf16),
            pltpu.VMEM((peers, heads_dev, out_rows, STAT_ROWS, 128), bf16),
            pltpu.VMEM((requests, steps, inner), bf16),
            pltpu.VMEM((requests, steps, nstate), bf16),
            pltpu.VMEM((requests, steps, inner), bf16),
            pltpu.VMEM((requests, steps, bc_cols), bf16),
            pltpu.VMEM((width, 2 * inner), bf16),
            pltpu.VMEM((width, bc_cols), bf16),
            pltpu.VMEM((inner, width), bf16),
            pltpu.VMEM((requests, nstate, inner), bf16),
            pltpu.VMEM((requests, 1, heads), f32),
            pltpu.SemaphoreType.DMA((heads_dev,)),
            pltpu.SemaphoreType.DMA((5,)),
            pltpu.SemaphoreType.DMA((5,)),
        ],
        compiler_params=pltpu.CompilerParams(vmem_limit_bytes=MIX_MIB * MIB),
        cost_estimate=pl.CostEstimate(flops=4 * 10**9, bytes_accessed=8 * MIB, transcendentals=10**6),
        name="mix",
    )(
        arrive,
        arrived,
        w_dt,
        conv_x_w,
        conv_bc_w,
        dt_bias[None, :],
        a_log[None, :],
        jnp.repeat(d_skip, headdim)[None, :],
        norm_gain[None, :],
        count_col,
        conv_x_state,
        conv_bc_state,
        in_hbm(w_zx.reshape(width, 2 * inner)),
        in_hbm(w_bc),
        in_hbm(w_out),
        in_hbm(turned),
    )
    leaving = leaving.reshape(peers * heads_dev, out_rows, STAT_ROWS, 128)
    returned = lax.all_to_all(leaving, ("req", "head"), split_axis=0, concat_axis=0, tiled=True)
    new_state, new_conv_x, new_conv_bc = pl.pallas_call(
        state_kernel,
        out_shape=(
            pltpu.HBM((requests, inner, nstate), f32),
            jax.ShapeDtypeStruct(conv_x_state.shape, f32),
            jax.ShapeDtypeStruct(conv_bc_state.shape, f32),
        ),
        in_specs=[smem()] + vmem(7) + hbm(1),
        out_specs=tuple(hbm(1) + vmem(2)),
        scratch_shapes=[
            pltpu.VMEM((requests, 8 + steps, inner), f32),
            pltpu.VMEM((requests, 8 + steps, bc_cols), f32),
            pltpu.VMEM((requests, inner, nstate), f32),
            pltpu.SemaphoreType.DMA((requests,)),
            pltpu.SemaphoreType.DMA((requests,)),
        ],
        compiler_params=pltpu.CompilerParams(vmem_limit_bytes=STATE_MIB * MIB),
        cost_estimate=pl.CostEstimate(flops=2 * 10**9, bytes_accessed=20 * MIB, transcendentals=0),
        name="update",
    )(arrive, push, b_conv, decay, x_in, bc_in, conv_x_state, conv_bc_state, states)
    out = pl.pallas_call(
        functools.partial(final_kernel, heads_dev=heads_dev, inner_all=inner * heads_dev),
        out_shape=jax.ShapeDtypeStruct((requests, steps, part), bf16),
        in_specs=[smem(), smem()] + vmem(1),
        out_specs=vmem(1)[0],
        scratch_shapes=[pltpu.SMEM((requests,), jnp.int32)],
        compiler_params=pltpu.CompilerParams(vmem_limit_bytes=4 * MIB),
        name="place_rows",
    )(slot, lengths, returned)
    return (out, new_state.reshape(ssm_state.shape), new_conv_x, new_conv_bc)


def solution(mesh):
    in_specs = (
        P("req", None, "head"),
        P(None, None, "head"),
        P(),
        P(None, "head"),
        P(None, "head"),
        P(),
        P("head"),
        P("head"),
        P("head"),
        P("head"),
        P("head", None),
        P("req", "head", None, None),
        P("req", None, "head"),
        P("req", None, None),
        P(),
        P(),
        P(),
    )
    out_specs = (
        P("req", None, "head"),
        P("req", "head", None, None),
        P("req", None, "head"),
        P("req", None, None),
    )
    return jax.shard_map(
        per_device, mesh=mesh, in_specs=in_specs, out_specs=out_specs, check_vma=False
    )
```

```python
import functools

import jax
import jax.numpy as jnp
from jax import lax
from jax.experimental import pallas as pl
from jax.experimental.pallas import tpu as pltpu
from jax.sharding import PartitionSpec as P

f32 = jnp.float32
bf16 = jnp.bfloat16
NT = (((1,), (1,)), ((), ()))
TN = (((0,), (0,)), ((), ()))
STAT_ROWS = 4
MIB = 1024 * 1024
MIX_MIB = 36
STAGE_MIB = 14
STATE_MIB = 16


def visit(slot_ref, first, requests, act):
    def body(i, met):
        owner = lax.div(slot_ref[first + i], requests)
        bit = lax.shift_left(jnp.int32(1), owner)
        act(i, owner, lax.min(met & bit, 1))
        return met | bit

    lax.fori_loop(0, requests, body, jnp.int32(0), unroll=8)


def send_kernel(slot_ref, hid_ref, out_hbm, buf, sem, *, heads_dev):
    requests = hid_ref.shape[0]
    peers = buf.shape[0] // (2 * heads_dev)

    def block(o):
        at = pl.ds(o * 2 * heads_dev, 2 * heads_dev)
        return pltpu.make_async_copy(buf.at[at], out_hbm.at[at], sem.at[o])

    def place(i, owner, j):
        rows = hid_ref[i]
        for h in range(heads_dev):
            buf[(owner * heads_dev + h) * 2 + j] = rows

        @pl.when(j == 1)
        def _():
            block(owner).start()

    visit(slot_ref, lax.axis_index("req") * requests, requests, place)
    lax.fori_loop(0, peers, lambda o, c: (block(o).wait(), c)[1], 0)


def stage_kernel(arrive, state_hbm, turned_hbm, st_ref, turned_ref, in_sem, out_sem):
    requests = turned_ref.shape[0]

    def load_state(i):
        return pltpu.make_async_copy(state_hbm.at[arrive[i]], st_ref.at[i], in_sem.at[i])

    def save(i):
        return pltpu.make_async_copy(turned_ref.at[i], turned_hbm.at[i], out_sem.at[i])

    lax.fori_loop(0, requests, lambda i, c: (load_state(i).start(), c)[1], 0)

    def body(i, carry):
        load_state(i).wait()
        turned_ref[i] = st_ref[i].astype(bf16).T
        save(i).start()
        return carry

    lax.fori_loop(0, requests, body, 0)
    lax.fori_loop(0, requests, lambda i, c: (save(i).wait(), c)[1], 0)


def split(x, terms):
    out = []
    for _ in range(terms - 1):
        out.append(x.astype(bf16))
        x = x - out[-1].astype(f32)
    return out + [x.astype(bf16)]


def mix_kernel(
    arrive,
    recv_ref,
    wdt_ref,
    cxw_ref,
    cbw_ref,
    bias_ref,
    alog_ref,
    skip_ref,
    gain_ref,
    cvec_ref,
    cx_ref,
    cb_ref,
    wzx_hbm,
    wbc_hbm,
    wout_hbm,
    turned_hbm,
    out_hbm,
    push_hbm,
    b_hbm,
    dec_hbm,
    xin_hbm,
    bin_hbm,
    xw_ref,
    bw_ref,
    gate_ref,
    ec_ref,
    sc_ref,
    fd_ref,
    g_ref,
    sq_ref,
    out_ref,
    push_ref,
    b_ref,
    xin_ref,
    bin_ref,
    wzx_ref,
    wbc_ref,
    wout_ref,
    turned_ref,
    dec_ref,
    out_sem,
    side_sem,
    weight_sem,
    *,
    heads_dev,
):
    requests = cx_ref.shape[0]
    tail = cx_ref.shape[1]
    inner = xw_ref.shape[2]
    steps = recv_ref.shape[1]
    part = recv_ref.shape[2]
    peers = recv_ref.shape[0] // (2 * heads_dev)
    tokens = requests * steps
    nstate = b_ref.shape[2]
    heads = wdt_ref.shape[1]
    headdim = inner // heads
    spread = heads * steps
    base = 8 - tail
    blk = 256
    blocks = inner // blk

    z_cols, x_cols = pl.ds(0, inner), pl.ds(inner, inner)
    load_x, load_bc, load_z, load_turned, load_out = [
        pltpu.make_async_copy(src, dst, weight_sem.at[n])
        for n, (src, dst) in enumerate(
            [
                (wzx_hbm.at[:, x_cols], wzx_ref.at[:, x_cols]),
                (wbc_hbm, wbc_ref),
                (wzx_hbm.at[:, z_cols], wzx_ref.at[:, z_cols]),
                (turned_hbm, turned_ref),
                (wout_hbm, wout_ref),
            ]
        )
    ]
    for copy in (load_x, load_bc, load_z, load_turned, load_out):
        copy.start()

    def previous(i, carry):
        row = arrive[i]
        xw_ref[i, base:8, :] = cx_ref[row]
        bw_ref[i, base:8, :] = cb_ref[row]
        return carry

    lax.fori_loop(0, requests, previous, 0, unroll=4)

    view = recv_ref.reshape(peers, heads_dev, 2, steps, part)
    def proj(w):
        half = peers // 2
        return jnp.concatenate(
            [
                jnp.dot(
                    jnp.concatenate(
                        [
                            view[k * half : (k + 1) * half, h].reshape(tokens // 2, part)
                            for h in range(heads_dev)
                        ],
                        axis=1,
                    ),
                    w,
                    preferred_element_type=f32,
                ).astype(bf16)
                for k in range(2)
            ],
            axis=0,
        )

    dt_in = proj(wdt_ref[...]).astype(f32)
    pre = dt_in + bias_ref[...]
    dt = jnp.maximum(pre, 0.0) + jnp.log1p(jnp.exp(-jnp.abs(pre)))
    rate = -dt * jnp.exp(alog_ref[...])
    place = lax.rem(lax.broadcasted_iota(jnp.int32, (tokens, heads), 0), steps)
    cumul = rate
    d = 1
    while d < steps:
        cumul = cumul + jnp.where(place >= d, pltpu.roll(cumul, d, 0), 0.0)
        d *= 2
    live = place < cvec_ref[...]
    last = place == cvec_ref[...] - 1
    total = jnp.sum(jnp.where(last, cumul, 0.0).reshape(requests, steps, heads), axis=1, keepdims=True)
    dec_ref[...] = jnp.exp(total)
    totals = jnp.broadcast_to(total, (requests, steps, heads)).reshape(tokens, heads)
    scaled = jnp.where(live, jnp.exp(jnp.where(live, totals - cumul, 0.0)) * dt, 0.0)

    def widen(x, width, each, terms):
        rows = lax.broadcasted_iota(jnp.int32, (heads, width), 0)
        cols = lax.div(lax.broadcasted_iota(jnp.int32, (heads, width), 1), each)
        pick = (rows == cols).astype(bf16)
        wide = None
        for term in split(x, terms):
            more = jnp.dot(term, pick, preferred_element_type=f32)
            wide = more if wide is None else wide + more
        return wide.reshape(requests, steps, width)

    ec_ref[...] = widen(jnp.exp(cumul), inner, headdim, 2)
    sc_ref[...] = widen(scaled, inner, headdim, 2)
    cum2 = widen(cumul, spread, steps, 3)
    dt2 = widen(dt, spread, steps, 2)
    t_at = lax.broadcasted_iota(jnp.int32, (1, steps, spread), 1)
    s_at = lax.rem(lax.broadcasted_iota(jnp.int32, (1, steps, spread), 2), steps)
    same = t_at == s_at
    lower = t_at >= s_at
    crow = jnp.sum(jnp.where(same, cum2, 0.0), axis=1, keepdims=True)
    drow = jnp.sum(jnp.where(same, dt2, 0.0), axis=1, keepdims=True)
    fd_ref[...] = jnp.where(lower, jnp.exp(jnp.where(lower, cum2 - crow, 0.0)) * drow, 0.0)

    load_x.wait()
    load_bc.wait()
    for n in range(blocks):
        cols = slice(n * blk, (n + 1) * blk)
        x_n = proj(wzx_ref[:, inner + n * blk : inner + (n + 1) * blk])
        xin_ref[:, :, cols] = x_n.reshape(requests, steps, blk)
        xw_ref[:, 8 : 8 + steps, cols] = x_n.astype(f32).reshape(requests, steps, blk)
    bc_n = proj(wbc_ref[...])
    bin_ref[...] = bc_n.reshape(requests, steps, 2 * nstate)
    bw_ref[:, 8 : 8 + steps, :] = bc_n.astype(f32).reshape(requests, steps, 2 * nstate)
    side = [
        pltpu.make_async_copy(xin_ref, xin_hbm, side_sem.at[0]),
        pltpu.make_async_copy(bin_ref, bin_hbm, side_sem.at[1]),
        pltpu.make_async_copy(push_ref, push_hbm, side_sem.at[2]),
        pltpu.make_async_copy(b_ref, b_hbm, side_sem.at[3]),
        pltpu.make_async_copy(dec_ref, dec_hbm, side_sem.at[4]),
    ]
    side[0].start()
    side[1].start()
    load_z.wait()
    for n in range(blocks):
        gate_ref[:, n * blk : (n + 1) * blk] = proj(wzx_ref[:, n * blk : (n + 1) * blk])

    group = heads // 2
    gspread, ginner = group * steps, group * headdim
    r_head = lax.div(lax.broadcasted_iota(jnp.int32, (gspread, ginner), 0), steps)
    c_head = lax.div(lax.broadcasted_iota(jnp.int32, (gspread, ginner), 1), headdim)
    diag = (r_head == c_head).astype(bf16)
    many = 16
    rows = many * steps
    own = lax.div(lax.broadcasted_iota(jnp.int32, (rows, rows), 0), steps) == lax.div(
        lax.broadcasted_iota(jnp.int32, (rows, rows), 1), steps
    )
    repeat = (
        lax.rem(lax.broadcasted_iota(jnp.int32, (rows, spread), 0), steps)
        == lax.rem(lax.broadcasted_iota(jnp.int32, (rows, spread), 1), steps)
    ).astype(bf16)

    def conv(win_ref, w_ref, at):
        total_c = w_ref[tail + 1 : tail + 2, :][None]
        for k in range(tail + 1):
            total_c = total_c + w_ref[k : k + 1, :][None] * win_ref[at, base + k : base + k + steps, :]
        return (total_c * lax.logistic(total_c)).astype(bf16)

    def body(n):
        at = slice(n * many, (n + 1) * many)
        x = conv(xw_ref, cxw_ref, at)
        bc = conv(bw_ref, cbw_ref, at)
        b_ref[at] = bc[:, :, :nstate]
        b = bc[:, :, :nstate].reshape(rows, nstate)
        c = bc[:, :, nstate:].reshape(rows, nstate)
        gram = jnp.where(own, lax.dot_general(c, b, NT, preferred_element_type=f32), 0.0)
        spread_gram = sum(jnp.dot(t, repeat, preferred_element_type=f32) for t in split(gram, 2))
        factor = (spread_gram * fd_ref[at].reshape(rows, spread)).astype(bf16)
        parts = []
        for r in range(many):
            tok_r = slice(r * steps, (r + 1) * steps)
            carried = jnp.dot(c[tok_r], turned_ref[n * many + r], preferred_element_type=f32)
            within = jnp.concatenate(
                [
                    jnp.dot(
                        factor[tok_r, g * gspread : (g + 1) * gspread],
                        jnp.concatenate([x[r, :, g * ginner : (g + 1) * ginner]] * group, axis=0)
                        * diag,
                        preferred_element_type=f32,
                    )
                    for g in range(2)
                ],
                axis=1,
            )
            parts.append(carried * ec_ref[n * many + r] + within)
        xf = x.astype(f32).reshape(rows, inner)
        mixed = (jnp.concatenate(parts, axis=0) + skip_ref[...] * xf).astype(bf16)
        push_ref[at] = (xf * sc_ref[at].reshape(rows, inner)).astype(bf16).reshape(many, steps, inner)
        tok_at = slice(n * rows, (n + 1) * rows)
        gate = gate_ref[tok_at, :].astype(f32)
        gated = mixed.astype(f32) * (gate * lax.logistic(gate))
        sq_ref[tok_at, :] = (gated * gated).astype(bf16)
        g_ref[tok_at, :] = (gated * gain_ref[...]).astype(bf16)

    load_turned.wait()
    load_out.wait()
    for n in range(requests // many):
        body(n)

    side[2].start()
    side[3].start()
    side[4].start()

    ones = jnp.ones((8, inner), bf16)
    squares = lax.dot_general(ones, sq_ref[...], NT, preferred_element_type=f32)
    high = squares.astype(bf16).astype(f32)
    first = lax.broadcasted_iota(jnp.int32, squares.shape, 0) == 0
    stats = jnp.where(first, high, squares - high).astype(bf16)
    pair = 2 * steps
    data_rows = 2 * pair

    def leave(h):
        return pltpu.make_async_copy(out_ref.at[:, h], out_hbm.at[:, h], out_sem.at[h])

    for b in range(peers):
        piece = jnp.concatenate(
            [stats[:STAT_ROWS, b * pair : (b + 1) * pair], jnp.zeros((STAT_ROWS, 128 - pair), bf16)], axis=1
        )
        for h in range(heads_dev):
            out_ref[b, h, data_rows // STAT_ROWS] = piece

    for h in range(heads_dev):
        cols = wout_ref[:, h * part : (h + 1) * part]
        res = jnp.concatenate(
            [
                jnp.dot(
                    g_ref[k * tokens // 2 : (k + 1) * tokens // 2, :], cols, preferred_element_type=f32
                ).astype(bf16)
                for k in range(2)
            ],
            axis=0,
        )
        part_rows = pair // STAT_ROWS
        out_ref[:, h, :part_rows] = res[:, :128].reshape(peers, part_rows, STAT_ROWS, 128)
        out_ref[:, h, part_rows : 2 * part_rows] = res[:, 128:].reshape(peers, part_rows, STAT_ROWS, 128)
        leave(h).start()
    for h in range(heads_dev):
        leave(h).wait()
    for copy in side:
        copy.wait()


def state_kernel(
    arrive,
    push_ref,
    b_ref,
    dec_ref,
    xin_ref,
    bin_ref,
    cx_ref,
    cb_ref,
    state_hbm,
    newstate_hbm,
    ncx_ref,
    ncb_ref,
    xw_ref,
    bw_ref,
    st_ref,
    in_sem,
    out_sem,
):
    requests, steps, inner = push_ref.shape
    tail = ncx_ref.shape[1]
    nstate = b_ref.shape[2]
    heads = dec_ref.shape[2]
    headdim = inner // heads
    base = 8 - tail

    def load_state(i):
        return pltpu.make_async_copy(state_hbm.at[arrive[i]], st_ref.at[i], in_sem.at[i])

    def save_state(i):
        return pltpu.make_async_copy(st_ref.at[i], newstate_hbm.at[arrive[i]], out_sem.at[i])

    lax.fori_loop(0, requests, lambda i, c: (load_state(i).start(), c)[1], 0)

    def body(i, carry):
        row = arrive[i]
        back = steps + tail - arrive[requests + i]
        xw_ref[i, base:8, :] = cx_ref[row]
        xw_ref[i, 8:, :] = xin_ref[i].astype(f32)
        bw_ref[i, base:8, :] = cb_ref[row]
        bw_ref[i, 8:, :] = bin_ref[i].astype(f32)
        ncx_ref[row] = pltpu.roll(xw_ref[i], back, 0)[:tail]
        ncb_ref[row] = pltpu.roll(bw_ref[i], back, 0)[:tail]
        update = lax.dot_general(push_ref[i], b_ref[i], TN, preferred_element_type=f32)
        dec = dec_ref[i]
        load_state(i).wait()
        for h in range(heads):
            sl = slice(h * headdim, (h + 1) * headdim)
            factor_h = jnp.broadcast_to(dec[:, h : h + 1], (headdim, nstate))
            st_ref[i, sl, :] = factor_h * st_ref[i, sl, :] + update[sl, :]
        save_state(i).start()
        return carry

    lax.fori_loop(0, requests, body, 0)
    lax.fori_loop(0, requests, lambda i, c: (save_state(i).wait(), c)[1], 0)


def final_kernel(slot_ref, len_ref, recv_ref, out_ref, order, *, heads_dev, inner_all):
    requests, steps, part = out_ref.shape
    peers = requests // 2
    pair = 2 * steps
    data_rows = 2 * pair
    base = lax.axis_index("req") * requests

    def note(i, owner, j):
        order[owner * 2 + j] = i

    visit(slot_ref, base, requests, note)
    groups = data_rows // STAT_ROWS
    view = recv_ref.reshape(peers, heads_dev, groups + 1, STAT_ROWS, 128)
    own = lax.broadcasted_iota(jnp.int32, (pair, 128), 0) == lax.broadcasted_iota(
        jnp.int32, (pair, 128), 1
    )
    place = lax.broadcasted_iota(jnp.int32, (steps, 128), 0)

    def body(o, carry):
        stats = view[o, 0, groups].astype(f32)
        acc = view[o, 0, :groups].astype(f32)
        for h in range(1, heads_dev):
            stats = stats + view[o, h, groups].astype(f32)
            acc = acc + view[o, h, :groups].astype(f32)
        acc = acc.reshape(data_rows, 128)
        squares = stats[0:1, :] + stats[1:2, :]
        total = jnp.sum(jnp.where(own, squares, 0.0), axis=1, keepdims=True)
        scale = lax.rsqrt(total / inner_all + 1e-05)
        for j in range(2):
            i = order[o * 2 + j]
            keep = place < len_ref[base + i]
            for half in range(2):
                at = half * pair + j * steps
                value = acc[at : at + steps, :] * scale[j * steps : (j + 1) * steps, :]
                out_ref[i, :, half * 128 : (half + 1) * 128] = jnp.where(keep, value, 0.0).astype(bf16)
        return carry

    lax.fori_loop(0, peers, body, 0, unroll=4)


def vmem(n):
    return [pl.BlockSpec(memory_space=pltpu.VMEM)] * n


def smem():
    return pl.BlockSpec(memory_space=pltpu.SMEM)


def hbm(n):
    return [pl.BlockSpec(memory_space=pltpu.HBM)] * n


def in_hbm(x):
    return pltpu.with_memory_space_constraint(x, pltpu.HBM)


def per_device(
    hidden,
    w_zx,
    w_bc,
    w_dt,
    conv_x_w,
    conv_bc_w,
    dt_bias,
    a_log,
    d_skip,
    norm_gain,
    w_out,
    ssm_state,
    conv_x_state,
    conv_bc_state,
    slot,
    lengths,
    accepted,
):
    requests, steps, part = hidden.shape
    width = w_zx.shape[0]
    inner = w_zx.shape[2]
    bc_cols = w_bc.shape[1]
    heads = w_dt.shape[1]
    headdim = inner // heads
    nstate = bc_cols // 2
    tail = conv_x_state.shape[1]
    peers = lax.axis_size("req")
    heads_dev = lax.axis_size("head")
    tokens = requests * steps
    spread = heads * steps
    out_rows = 4 * steps // STAT_ROWS + 1
    me = lax.axis_index("req")

    slot_blocks = slot.reshape(peers, requests)
    outgoing = pl.pallas_call(
        functools.partial(send_kernel, heads_dev=heads_dev),
        out_shape=pltpu.HBM((peers * heads_dev * 2, steps, part), bf16),
        in_specs=[smem()] + vmem(1),
        out_specs=hbm(1)[0],
        scratch_shapes=[
            pltpu.VMEM((peers * heads_dev * 2, steps, part), bf16),
            pltpu.SemaphoreType.DMA((peers,)),
        ],
        compiler_params=pltpu.CompilerParams(vmem_limit_bytes=4 * MIB),
        name="send_rows",
    )(in_hbm(slot), in_hbm(hidden))
    arrived = lax.all_to_all(outgoing, ("req", "head"), split_axis=0, concat_axis=0, tiled=True)

    counted = jnp.minimum(accepted, lengths).reshape(peers, requests)
    order = jnp.arange(requests, dtype=jnp.int32)[None, :]
    code = (order * requests + slot_blocks % requests) * (2 * steps) + counted
    here = slot_blocks // requests == me
    low = jnp.min(jnp.where(here, code, jnp.iinfo(jnp.int32).max), axis=1)
    high = jnp.max(jnp.where(here, code, -1), axis=1)
    both = jnp.stack([low, high], axis=1).reshape(requests)
    rows = (both // (2 * steps)) % requests
    counts = both % (2 * steps)
    arrive = jnp.concatenate([rows, counts])
    count_col = jnp.broadcast_to(counts[:, None, None], (requests, steps, heads)).reshape(tokens, heads)

    states = in_hbm(ssm_state.reshape(requests, inner, nstate))
    turned = pl.pallas_call(
        stage_kernel,
        out_shape=pltpu.HBM((requests, nstate, inner), bf16),
        in_specs=[smem()] + hbm(1),
        out_specs=hbm(1)[0],
        scratch_shapes=[
            pltpu.VMEM((requests, inner, nstate), f32),
            pltpu.VMEM((requests, nstate, inner), bf16),
            pltpu.SemaphoreType.DMA((requests,)),
            pltpu.SemaphoreType.DMA((requests,)),
        ],
        compiler_params=pltpu.CompilerParams(vmem_limit_bytes=STAGE_MIB * MIB),
        cost_estimate=pl.CostEstimate(flops=10**9, bytes_accessed=20 * MIB, transcendentals=0),
        name="stage",
    )(arrive, states)
    leaving, push, b_conv, decay, x_in, bc_in = pl.pallas_call(
        functools.partial(mix_kernel, heads_dev=heads_dev),
        out_shape=(
            pltpu.HBM((peers, heads_dev, out_rows, STAT_ROWS, 128), bf16),
            pltpu.HBM((requests, steps, inner), bf16),
            pltpu.HBM((requests, steps, nstate), bf16),
            pltpu.HBM((requests, 1, heads), f32),
            pltpu.HBM((requests, steps, inner), bf16),
            pltpu.HBM((requests, steps, bc_cols), bf16),
        ),
        in_specs=[smem()] + vmem(11) + hbm(4),
        out_specs=tuple(hbm(6)),
        scratch_shapes=[
            pltpu.VMEM((requests, 8 + steps, inner), f32),
            pltpu.VMEM((requests, 8 + steps, bc_cols), f32),
            pltpu.VMEM((tokens, inner), bf16),
            pltpu.VMEM((requests, steps, inner), f32),
            pltpu.VMEM((requests, steps, inner), f32),
            pltpu.VMEM((requests, steps, spread), f32),
            pltpu.VMEM((tokens, inner), bf16),
            pltpu.VMEM((tokens, inner), bf16),
            pltpu.VMEM((peers, heads_dev, out_rows, STAT_ROWS, 128), bf16),
            pltpu.VMEM((requests, steps, inner), bf16),
            pltpu.VMEM((requests, steps, nstate), bf16),
            pltpu.VMEM((requests, steps, inner), bf16),
            pltpu.VMEM((requests, steps, bc_cols), bf16),
            pltpu.VMEM((width, 2 * inner), bf16),
            pltpu.VMEM((width, bc_cols), bf16),
            pltpu.VMEM((inner, width), bf16),
            pltpu.VMEM((requests, nstate, inner), bf16),
            pltpu.VMEM((requests, 1, heads), f32),
            pltpu.SemaphoreType.DMA((heads_dev,)),
            pltpu.SemaphoreType.DMA((5,)),
            pltpu.SemaphoreType.DMA((5,)),
        ],
        compiler_params=pltpu.CompilerParams(vmem_limit_bytes=MIX_MIB * MIB),
        cost_estimate=pl.CostEstimate(flops=4 * 10**9, bytes_accessed=8 * MIB, transcendentals=10**6),
        name="mix",
    )(
        arrive,
        arrived,
        w_dt,
        conv_x_w,
        conv_bc_w,
        dt_bias[None, :],
        a_log[None, :],
        jnp.repeat(d_skip, headdim)[None, :],
        norm_gain[None, :],
        count_col,
        conv_x_state,
        conv_bc_state,
        in_hbm(w_zx.reshape(width, 2 * inner)),
        in_hbm(w_bc),
        in_hbm(w_out),
        in_hbm(turned),
    )
    leaving = leaving.reshape(peers * heads_dev, out_rows, STAT_ROWS, 128)
    returned = lax.all_to_all(leaving, ("req", "head"), split_axis=0, concat_axis=0, tiled=True)
    new_state, new_conv_x, new_conv_bc = pl.pallas_call(
        state_kernel,
        out_shape=(
            pltpu.HBM((requests, inner, nstate), f32),
            jax.ShapeDtypeStruct(conv_x_state.shape, f32),
            jax.ShapeDtypeStruct(conv_bc_state.shape, f32),
        ),
        in_specs=[smem()] + vmem(7) + hbm(1),
        out_specs=tuple(hbm(1) + vmem(2)),
        scratch_shapes=[
            pltpu.VMEM((requests, 8 + steps, inner), f32),
            pltpu.VMEM((requests, 8 + steps, bc_cols), f32),
            pltpu.VMEM((requests, inner, nstate), f32),
            pltpu.SemaphoreType.DMA((requests,)),
            pltpu.SemaphoreType.DMA((requests,)),
        ],
        compiler_params=pltpu.CompilerParams(vmem_limit_bytes=STATE_MIB * MIB),
        cost_estimate=pl.CostEstimate(flops=2 * 10**9, bytes_accessed=20 * MIB, transcendentals=0),
        name="update",
    )(arrive, push, b_conv, decay, x_in, bc_in, conv_x_state, conv_bc_state, states)
    out = pl.pallas_call(
        functools.partial(final_kernel, heads_dev=heads_dev, inner_all=inner * heads_dev),
        out_shape=jax.ShapeDtypeStruct((requests, steps, part), bf16),
        in_specs=[smem(), smem()] + vmem(1),
        out_specs=vmem(1)[0],
        scratch_shapes=[pltpu.SMEM((requests,), jnp.int32)],
        compiler_params=pltpu.CompilerParams(vmem_limit_bytes=4 * MIB),
        name="place_rows",
    )(slot, lengths, returned)
    return (out, new_state.reshape(ssm_state.shape), new_conv_x, new_conv_bc)


def solution(mesh):
    in_specs = (
        P("req", None, "head"),
        P(None, None, "head"),
        P(),
        P(None, "head"),
        P(None, "head"),
        P(),
        P("head"),
        P("head"),
        P("head"),
        P("head"),
        P("head", None),
        P("req", "head", None, None),
        P("req", None, "head"),
        P("req", None, None),
        P(),
        P(),
        P(),
    )
    out_specs = (
        P("req", None, "head"),
        P("req", "head", None, None),
        P("req", None, "head"),
        P("req", None, None),
    )
    return jax.shard_map(
        per_device, mesh=mesh, in_specs=in_specs, out_specs=out_specs, check_vma=False
    )
```

```python
import functools

import jax
import jax.numpy as jnp
from jax import lax
from jax.experimental import pallas as pl
from jax.experimental.pallas import tpu as pltpu
from jax.sharding import PartitionSpec as P

f32 = jnp.float32
bf16 = jnp.bfloat16
NT = (((1,), (1,)), ((), ()))
TN = (((0,), (0,)), ((), ()))
STAT_ROWS = 4
MIB = 1024 * 1024
MIX_MIB = 36
STAGE_MIB = 14
STATE_MIB = 16


def visit(slot_ref, first, requests, act):
    def body(i, met):
        owner = lax.div(slot_ref[first + i], requests)
        bit = lax.shift_left(jnp.int32(1), owner)
        act(i, owner, lax.min(met & bit, 1))
        return met | bit

    lax.fori_loop(0, requests, body, jnp.int32(0), unroll=8)


def send_kernel(slot_ref, hid_ref, out_hbm, buf, sem, *, heads_dev):
    requests = hid_ref.shape[0]
    peers = buf.shape[0] // (2 * heads_dev)

    def block(o):
        at = pl.ds(o * 2 * heads_dev, 2 * heads_dev)
        return pltpu.make_async_copy(buf.at[at], out_hbm.at[at], sem.at[o])

    def place(i, owner, j):
        rows = hid_ref[i]
        for h in range(heads_dev):
            buf[(owner * heads_dev + h) * 2 + j] = rows

        @pl.when(j == 1)
        def _():
            block(owner).start()

    visit(slot_ref, lax.axis_index("req") * requests, requests, place)
    lax.fori_loop(0, peers, lambda o, c: (block(o).wait(), c)[1], 0)


def stage_kernel(arrive, state_hbm, turned_hbm, st_ref, turned_ref, in_sem, out_sem):
    requests = turned_ref.shape[0]

    def load_state(i):
        return pltpu.make_async_copy(state_hbm.at[arrive[i]], st_ref.at[i], in_sem.at[i])

    def save(i):
        return pltpu.make_async_copy(turned_ref.at[i], turned_hbm.at[i], out_sem.at[i])

    lax.fori_loop(0, requests, lambda i, c: (load_state(i).start(), c)[1], 0)

    def body(i, carry):
        load_state(i).wait()
        turned_ref[i] = st_ref[i].astype(bf16).T
        save(i).start()
        return carry

    lax.fori_loop(0, requests, body, 0)
    lax.fori_loop(0, requests, lambda i, c: (save(i).wait(), c)[1], 0)


def split(x, terms):
    out = []
    for _ in range(terms - 1):
        out.append(x.astype(bf16))
        x = x - out[-1].astype(f32)
    return out + [x.astype(bf16)]


def mix_kernel(
    arrive,
    recv_ref,
    wdt_ref,
    cxw_ref,
    cbw_ref,
    bias_ref,
    alog_ref,
    skip_ref,
    gain_ref,
    cx_ref,
    cb_ref,
    wzx_hbm,
    wbc_hbm,
    wout_hbm,
    turned_hbm,
    out_hbm,
    push_hbm,
    b_hbm,
    dec_hbm,
    xin_hbm,
    bin_hbm,
    xw_ref,
    bw_ref,
    gate_ref,
    ec_ref,
    sc_ref,
    fd_ref,
    g_ref,
    sq_ref,
    out_ref,
    push_ref,
    b_ref,
    xin_ref,
    bin_ref,
    wzx_ref,
    wbc_ref,
    wout_ref,
    turned_ref,
    dec_ref,
    cvec_ref,
    out_sem,
    side_sem,
    weight_sem,
    *,
    heads_dev,
):
    requests = cx_ref.shape[0]
    tail = cx_ref.shape[1]
    inner = xw_ref.shape[2]
    steps = recv_ref.shape[1]
    part = recv_ref.shape[2]
    peers = recv_ref.shape[0] // (2 * heads_dev)
    tokens = requests * steps
    nstate = b_ref.shape[2]
    heads = wdt_ref.shape[1]
    headdim = inner // heads
    spread = heads * steps
    base = 8 - tail
    blk = 256
    blocks = inner // blk

    z_cols, x_cols = pl.ds(0, inner), pl.ds(inner, inner)
    load_x, load_bc, load_z, load_turned, load_out = [
        pltpu.make_async_copy(src, dst, weight_sem.at[n])
        for n, (src, dst) in enumerate(
            [
                (wzx_hbm.at[:, x_cols], wzx_ref.at[:, x_cols]),
                (wbc_hbm, wbc_ref),
                (wzx_hbm.at[:, z_cols], wzx_ref.at[:, z_cols]),
                (turned_hbm, turned_ref),
                (wout_hbm, wout_ref),
            ]
        )
    ]
    for copy in (load_x, load_bc, load_z, load_turned, load_out):
        copy.start()

    def previous(i, carry):
        row = arrive[i]
        xw_ref[i, base:8, :] = cx_ref[row]
        bw_ref[i, base:8, :] = cb_ref[row]
        tok_at = pl.ds(pl.multiple_of(i * steps, steps), steps)
        cvec_ref[tok_at, :] = jnp.full((steps, heads), arrive[requests + i], jnp.int32)
        return carry

    lax.fori_loop(0, requests, previous, 0, unroll=4)

    view = recv_ref.reshape(peers, heads_dev, 2, steps, part)
    def proj(w):
        half = peers // 2
        return jnp.concatenate(
            [
                jnp.dot(
                    jnp.concatenate(
                        [
                            view[k * half : (k + 1) * half, h].reshape(tokens // 2, part)
                            for h in range(heads_dev)
                        ],
                        axis=1,
                    ),
                    w,
                    preferred_element_type=f32,
                ).astype(bf16)
                for k in range(2)
            ],
            axis=0,
        )

    dt_in = proj(wdt_ref[...]).astype(f32)
    pre = dt_in + bias_ref[...]
    dt = jnp.maximum(pre, 0.0) + jnp.log1p(jnp.exp(-jnp.abs(pre)))
    rate = -dt * jnp.exp(alog_ref[...])
    place = lax.rem(lax.broadcasted_iota(jnp.int32, (tokens, heads), 0), steps)
    cumul = rate
    d = 1
    while d < steps:
        cumul = cumul + jnp.where(place >= d, pltpu.roll(cumul, d, 0), 0.0)
        d *= 2
    live = place < cvec_ref[...]
    last = place == cvec_ref[...] - 1
    total = jnp.sum(jnp.where(last, cumul, 0.0).reshape(requests, steps, heads), axis=1, keepdims=True)
    dec_ref[...] = jnp.exp(total)
    totals = jnp.broadcast_to(total, (requests, steps, heads)).reshape(tokens, heads)
    scaled = jnp.where(live, jnp.exp(jnp.where(live, totals - cumul, 0.0)) * dt, 0.0)

    def widen(x, width, each, terms):
        rows = lax.broadcasted_iota(jnp.int32, (heads, width), 0)
        cols = lax.div(lax.broadcasted_iota(jnp.int32, (heads, width), 1), each)
        pick = (rows == cols).astype(bf16)
        wide = None
        for term in split(x, terms):
            more = jnp.dot(term, pick, preferred_element_type=f32)
            wide = more if wide is None else wide + more
        return wide.reshape(requests, steps, width)

    ec_ref[...] = widen(jnp.exp(cumul), inner, headdim, 2)
    sc_ref[...] = widen(scaled, inner, headdim, 2)
    cum2 = widen(cumul, spread, steps, 3)
    dt2 = widen(dt, spread, steps, 2)
    t_at = lax.broadcasted_iota(jnp.int32, (1, steps, spread), 1)
    s_at = lax.rem(lax.broadcasted_iota(jnp.int32, (1, steps, spread), 2), steps)
    same = t_at == s_at
    lower = t_at >= s_at
    crow = jnp.sum(jnp.where(same, cum2, 0.0), axis=1, keepdims=True)
    drow = jnp.sum(jnp.where(same, dt2, 0.0), axis=1, keepdims=True)
    fd_ref[...] = jnp.where(lower, jnp.exp(jnp.where(lower, cum2 - crow, 0.0)) * drow, 0.0)

    load_x.wait()
    load_bc.wait()
    for n in range(blocks):
        cols = slice(n * blk, (n + 1) * blk)
        x_n = proj(wzx_ref[:, inner + n * blk : inner + (n + 1) * blk])
        xin_ref[:, :, cols] = x_n.reshape(requests, steps, blk)
        xw_ref[:, 8 : 8 + steps, cols] = x_n.astype(f32).reshape(requests, steps, blk)
    bc_n = proj(wbc_ref[...])
    bin_ref[...] = bc_n.reshape(requests, steps, 2 * nstate)
    bw_ref[:, 8 : 8 + steps, :] = bc_n.astype(f32).reshape(requests, steps, 2 * nstate)
    side = [
        pltpu.make_async_copy(xin_ref, xin_hbm, side_sem.at[0]),
        pltpu.make_async_copy(bin_ref, bin_hbm, side_sem.at[1]),
        pltpu.make_async_copy(push_ref, push_hbm, side_sem.at[2]),
        pltpu.make_async_copy(b_ref, b_hbm, side_sem.at[3]),
        pltpu.make_async_copy(dec_ref, dec_hbm, side_sem.at[4]),
    ]
    side[0].start()
    side[1].start()
    load_z.wait()
    for n in range(blocks):
        gate_ref[:, n * blk : (n + 1) * blk] = proj(wzx_ref[:, n * blk : (n + 1) * blk])

    group = heads // 2
    gspread, ginner = group * steps, group * headdim
    r_head = lax.div(lax.broadcasted_iota(jnp.int32, (gspread, ginner), 0), steps)
    c_head = lax.div(lax.broadcasted_iota(jnp.int32, (gspread, ginner), 1), headdim)
    diag = (r_head == c_head).astype(bf16)
    many = 16
    rows = many * steps
    own = lax.div(lax.broadcasted_iota(jnp.int32, (rows, rows), 0), steps) == lax.div(
        lax.broadcasted_iota(jnp.int32, (rows, rows), 1), steps
    )
    repeat = (
        lax.rem(lax.broadcasted_iota(jnp.int32, (rows, spread), 0), steps)
        == lax.rem(lax.broadcasted_iota(jnp.int32, (rows, spread), 1), steps)
    ).astype(bf16)

    def conv(win_ref, w_ref, at):
        total_c = w_ref[tail + 1 : tail + 2, :][None]
        for k in range(tail + 1):
            total_c = total_c + w_ref[k : k + 1, :][None] * win_ref[at, base + k : base + k + steps, :]
        return (total_c * lax.logistic(total_c)).astype(bf16)

    def body(n):
        at = slice(n * many, (n + 1) * many)
        x = conv(xw_ref, cxw_ref, at)
        bc = conv(bw_ref, cbw_ref, at)
        b_ref[at] = bc[:, :, :nstate]
        b = bc[:, :, :nstate].reshape(rows, nstate)
        c = bc[:, :, nstate:].reshape(rows, nstate)
        gram = jnp.where(own, lax.dot_general(c, b, NT, preferred_element_type=f32), 0.0)
        spread_gram = sum(jnp.dot(t, repeat, preferred_element_type=f32) for t in split(gram, 2))
        factor = (spread_gram * fd_ref[at].reshape(rows, spread)).astype(bf16)
        parts = []
        for r in range(many):
            tok_r = slice(r * steps, (r + 1) * steps)
            carried = jnp.dot(c[tok_r], turned_ref[n * many + r], preferred_element_type=f32)
            within = jnp.concatenate(
                [
                    jnp.dot(
                        factor[tok_r, g * gspread : (g + 1) * gspread],
                        jnp.concatenate([x[r, :, g * ginner : (g + 1) * ginner]] * group, axis=0)
                        * diag,
                        preferred_element_type=f32,
                    )
                    for g in range(2)
                ],
                axis=1,
            )
            parts.append(carried * ec_ref[n * many + r] + within)
        xf = x.astype(f32).reshape(rows, inner)
        mixed = (jnp.concatenate(parts, axis=0) + skip_ref[...] * xf).astype(bf16)
        push_ref[at] = (xf * sc_ref[at].reshape(rows, inner)).astype(bf16).reshape(many, steps, inner)
        tok_at = slice(n * rows, (n + 1) * rows)
        gate = gate_ref[tok_at, :].astype(f32)
        gated = mixed.astype(f32) * (gate * lax.logistic(gate))
        sq_ref[tok_at, :] = (gated * gated).astype(bf16)
        g_ref[tok_at, :] = (gated * gain_ref[...]).astype(bf16)

    load_turned.wait()
    load_out.wait()
    for n in range(requests // many):
        body(n)

    side[2].start()
    side[3].start()
    side[4].start()

    ones = jnp.ones((8, inner), bf16)
    squares = lax.dot_general(ones, sq_ref[...], NT, preferred_element_type=f32)
    high = squares.astype(bf16).astype(f32)
    first = lax.broadcasted_iota(jnp.int32, squares.shape, 0) == 0
    stats = jnp.where(first, high, squares - high).astype(bf16)
    pair = 2 * steps
    data_rows = 2 * pair

    def leave(h):
        return pltpu.make_async_copy(out_ref.at[:, h], out_hbm.at[:, h], out_sem.at[h])

    for b in range(peers):
        piece = jnp.concatenate(
            [stats[:STAT_ROWS, b * pair : (b + 1) * pair], jnp.zeros((STAT_ROWS, 128 - pair), bf16)], axis=1
        )
        for h in range(heads_dev):
            out_ref[b, h, data_rows // STAT_ROWS] = piece

    for h in range(heads_dev):
        cols = wout_ref[:, h * part : (h + 1) * part]
        res = jnp.concatenate(
            [
                jnp.dot(
                    g_ref[k * tokens // 2 : (k + 1) * tokens // 2, :], cols, preferred_element_type=f32
                ).astype(bf16)
                for k in range(2)
            ],
            axis=0,
        )
        part_rows = pair // STAT_ROWS
        out_ref[:, h, :part_rows] = res[:, :128].reshape(peers, part_rows, STAT_ROWS, 128)
        out_ref[:, h, part_rows : 2 * part_rows] = res[:, 128:].reshape(peers, part_rows, STAT_ROWS, 128)
        leave(h).start()
    for h in range(heads_dev):
        leave(h).wait()
    for copy in side:
        copy.wait()


def state_kernel(
    arrive,
    push_ref,
    b_ref,
    dec_ref,
    xin_ref,
    bin_ref,
    cx_ref,
    cb_ref,
    state_hbm,
    newstate_hbm,
    ncx_ref,
    ncb_ref,
    xw_ref,
    bw_ref,
    st_ref,
    in_sem,
    out_sem,
):
    requests, steps, inner = push_ref.shape
    tail = ncx_ref.shape[1]
    nstate = b_ref.shape[2]
    heads = dec_ref.shape[2]
    headdim = inner // heads
    base = 8 - tail

    def load_state(i):
        return pltpu.make_async_copy(state_hbm.at[arrive[i]], st_ref.at[i], in_sem.at[i])

    def save_state(i):
        return pltpu.make_async_copy(st_ref.at[i], newstate_hbm.at[arrive[i]], out_sem.at[i])

    lax.fori_loop(0, requests, lambda i, c: (load_state(i).start(), c)[1], 0)

    def body(i, carry):
        row = arrive[i]
        back = steps + tail - arrive[requests + i]
        xw_ref[i, base:8, :] = cx_ref[row]
        xw_ref[i, 8:, :] = xin_ref[i].astype(f32)
        bw_ref[i, base:8, :] = cb_ref[row]
        bw_ref[i, 8:, :] = bin_ref[i].astype(f32)
        ncx_ref[row] = pltpu.roll(xw_ref[i], back, 0)[:tail]
        ncb_ref[row] = pltpu.roll(bw_ref[i], back, 0)[:tail]
        update = lax.dot_general(push_ref[i], b_ref[i], TN, preferred_element_type=f32)
        dec = dec_ref[i]
        load_state(i).wait()
        for h in range(heads):
            sl = slice(h * headdim, (h + 1) * headdim)
            factor_h = jnp.broadcast_to(dec[:, h : h + 1], (headdim, nstate))
            st_ref[i, sl, :] = factor_h * st_ref[i, sl, :] + update[sl, :]
        save_state(i).start()
        return carry

    lax.fori_loop(0, requests, body, 0)
    lax.fori_loop(0, requests, lambda i, c: (save_state(i).wait(), c)[1], 0)


def final_kernel(info, recv_ref, out_ref, order, *, heads_dev, inner_all):
    requests, steps, part = out_ref.shape
    peers = requests // 2
    pair = 2 * steps
    data_rows = 2 * pair

    def note(i, owner, j):
        order[owner * 2 + j] = i

    visit(info, 0, requests, note)
    groups = data_rows // STAT_ROWS
    view = recv_ref.reshape(peers, heads_dev, groups + 1, STAT_ROWS, 128)
    own = lax.broadcasted_iota(jnp.int32, (pair, 128), 0) == lax.broadcasted_iota(
        jnp.int32, (pair, 128), 1
    )
    place = lax.broadcasted_iota(jnp.int32, (steps, 128), 0)

    def body(o, carry):
        stats = view[o, 0, groups].astype(f32)
        acc = view[o, 0, :groups].astype(f32)
        for h in range(1, heads_dev):
            stats = stats + view[o, h, groups].astype(f32)
            acc = acc + view[o, h, :groups].astype(f32)
        acc = acc.reshape(data_rows, 128)
        squares = stats[0:1, :] + stats[1:2, :]
        total = jnp.sum(jnp.where(own, squares, 0.0), axis=1, keepdims=True)
        scale = lax.rsqrt(total / inner_all + 1e-05)
        for j in range(2):
            i = order[o * 2 + j]
            keep = place < info[requests + i]
            for half in range(2):
                at = half * pair + j * steps
                value = acc[at : at + steps, :] * scale[j * steps : (j + 1) * steps, :]
                out_ref[i, :, half * 128 : (half + 1) * 128] = jnp.where(keep, value, 0.0).astype(bf16)
        return carry

    lax.fori_loop(0, peers, body, 0, unroll=4)


def vmem(n):
    return [pl.BlockSpec(memory_space=pltpu.VMEM)] * n


def smem():
    return pl.BlockSpec(memory_space=pltpu.SMEM)


def hbm(n):
    return [pl.BlockSpec(memory_space=pltpu.HBM)] * n


def in_hbm(x):
    return pltpu.with_memory_space_constraint(x, pltpu.HBM)


def per_device(
    hidden,
    w_zx,
    w_bc,
    w_dt,
    conv_x_w,
    conv_bc_w,
    dt_bias,
    a_log,
    d_skip,
    norm_gain,
    w_out,
    ssm_state,
    conv_x_state,
    conv_bc_state,
    slot,
    lengths,
    accepted,
):
    requests, steps, part = hidden.shape
    width = w_zx.shape[0]
    inner = w_zx.shape[2]
    bc_cols = w_bc.shape[1]
    heads = w_dt.shape[1]
    headdim = inner // heads
    nstate = bc_cols // 2
    tail = conv_x_state.shape[1]
    peers = lax.axis_size("req")
    heads_dev = lax.axis_size("head")
    tokens = requests * steps
    spread = heads * steps
    out_rows = 4 * steps // STAT_ROWS + 1
    me = lax.axis_index("req")

    slot_blocks = slot.reshape(peers, requests)
    outgoing = pl.pallas_call(
        functools.partial(send_kernel, heads_dev=heads_dev),
        out_shape=pltpu.HBM((peers * heads_dev * 2, steps, part), bf16),
        in_specs=[smem()] + vmem(1),
        out_specs=hbm(1)[0],
        scratch_shapes=[
            pltpu.VMEM((peers * heads_dev * 2, steps, part), bf16),
            pltpu.SemaphoreType.DMA((peers,)),
        ],
        compiler_params=pltpu.CompilerParams(vmem_limit_bytes=4 * MIB),
        name="send_rows",
    )(in_hbm(slot), in_hbm(hidden))
    arrived = lax.all_to_all(outgoing, ("req", "head"), split_axis=0, concat_axis=0, tiled=True)

    counted = jnp.minimum(accepted, lengths).reshape(peers, requests)
    order = jnp.arange(requests, dtype=jnp.int32)[None, :]
    code = (order * requests + slot_blocks % requests) * (2 * steps) + counted
    here = slot_blocks // requests == me
    low = jnp.min(jnp.where(here, code, jnp.iinfo(jnp.int32).max), axis=1)
    high = jnp.max(jnp.where(here, code, -1), axis=1)
    both = jnp.stack([low, high], axis=1).reshape(requests)
    rows = (both // (2 * steps)) % requests
    counts = both % (2 * steps)
    arrive = jnp.concatenate([rows, counts])

    states = in_hbm(ssm_state.reshape(requests, inner, nstate))
    turned = pl.pallas_call(
        stage_kernel,
        out_shape=pltpu.HBM((requests, nstate, inner), bf16),
        in_specs=[smem()] + hbm(1),
        out_specs=hbm(1)[0],
        scratch_shapes=[
            pltpu.VMEM((requests, inner, nstate), f32),
            pltpu.VMEM((requests, nstate, inner), bf16),
            pltpu.SemaphoreType.DMA((requests,)),
            pltpu.SemaphoreType.DMA((requests,)),
        ],
        compiler_params=pltpu.CompilerParams(vmem_limit_bytes=STAGE_MIB * MIB),
        cost_estimate=pl.CostEstimate(flops=10**9, bytes_accessed=20 * MIB, transcendentals=0),
        name="stage",
    )(arrive, states)
    leaving, push, b_conv, decay, x_in, bc_in = pl.pallas_call(
        functools.partial(mix_kernel, heads_dev=heads_dev),
        out_shape=(
            pltpu.HBM((peers, heads_dev, out_rows, STAT_ROWS, 128), bf16),
            pltpu.HBM((requests, steps, inner), bf16),
            pltpu.HBM((requests, steps, nstate), bf16),
            pltpu.HBM((requests, 1, heads), f32),
            pltpu.HBM((requests, steps, inner), bf16),
            pltpu.HBM((requests, steps, bc_cols), bf16),
        ),
        in_specs=[smem()] + vmem(10) + hbm(4),
        out_specs=tuple(hbm(6)),
        scratch_shapes=[
            pltpu.VMEM((requests, 8 + steps, inner), f32),
            pltpu.VMEM((requests, 8 + steps, bc_cols), f32),
            pltpu.VMEM((tokens, inner), bf16),
            pltpu.VMEM((requests, steps, inner), f32),
            pltpu.VMEM((requests, steps, inner), f32),
            pltpu.VMEM((requests, steps, spread), f32),
            pltpu.VMEM((tokens, inner), bf16),
            pltpu.VMEM((tokens, inner), bf16),
            pltpu.VMEM((peers, heads_dev, out_rows, STAT_ROWS, 128), bf16),
            pltpu.VMEM((requests, steps, inner), bf16),
            pltpu.VMEM((requests, steps, nstate), bf16),
            pltpu.VMEM((requests, steps, inner), bf16),
            pltpu.VMEM((requests, steps, bc_cols), bf16),
            pltpu.VMEM((width, 2 * inner), bf16),
            pltpu.VMEM((width, bc_cols), bf16),
            pltpu.VMEM((inner, width), bf16),
            pltpu.VMEM((requests, nstate, inner), bf16),
            pltpu.VMEM((requests, 1, heads), f32),
            pltpu.VMEM((tokens, heads), jnp.int32),
            pltpu.SemaphoreType.DMA((heads_dev,)),
            pltpu.SemaphoreType.DMA((5,)),
            pltpu.SemaphoreType.DMA((5,)),
        ],
        compiler_params=pltpu.CompilerParams(vmem_limit_bytes=MIX_MIB * MIB),
        cost_estimate=pl.CostEstimate(flops=4 * 10**9, bytes_accessed=8 * MIB, transcendentals=10**6),
        name="mix",
    )(
        arrive,
        arrived,
        w_dt,
        conv_x_w,
        conv_bc_w,
        dt_bias[None, :],
        a_log[None, :],
        jnp.repeat(d_skip, headdim)[None, :],
        norm_gain[None, :],
        conv_x_state,
        conv_bc_state,
        in_hbm(w_zx.reshape(width, 2 * inner)),
        in_hbm(w_bc),
        in_hbm(w_out),
        in_hbm(turned),
    )
    leaving = leaving.reshape(peers * heads_dev, out_rows, STAT_ROWS, 128)
    returned = lax.all_to_all(leaving, ("req", "head"), split_axis=0, concat_axis=0, tiled=True)
    new_state, new_conv_x, new_conv_bc = pl.pallas_call(
        state_kernel,
        out_shape=(
            pltpu.HBM((requests, inner, nstate), f32),
            jax.ShapeDtypeStruct(conv_x_state.shape, f32),
            jax.ShapeDtypeStruct(conv_bc_state.shape, f32),
        ),
        in_specs=[smem()] + vmem(7) + hbm(1),
        out_specs=tuple(hbm(1) + vmem(2)),
        scratch_shapes=[
            pltpu.VMEM((requests, 8 + steps, inner), f32),
            pltpu.VMEM((requests, 8 + steps, bc_cols), f32),
            pltpu.VMEM((requests, inner, nstate), f32),
            pltpu.SemaphoreType.DMA((requests,)),
            pltpu.SemaphoreType.DMA((requests,)),
        ],
        compiler_params=pltpu.CompilerParams(vmem_limit_bytes=STATE_MIB * MIB),
        cost_estimate=pl.CostEstimate(flops=2 * 10**9, bytes_accessed=20 * MIB, transcendentals=0),
        name="update",
    )(arrive, push, b_conv, decay, x_in, bc_in, conv_x_state, conv_bc_state, states)
    mine = jnp.concatenate(
        [
            lax.dynamic_slice_in_dim(slot, me * requests, requests),
            lax.dynamic_slice_in_dim(lengths, me * requests, requests),
        ]
    )
    out = pl.pallas_call(
        functools.partial(final_kernel, heads_dev=heads_dev, inner_all=inner * heads_dev),
        out_shape=jax.ShapeDtypeStruct((requests, steps, part), bf16),
        in_specs=[smem()] + vmem(1),
        out_specs=vmem(1)[0],
        scratch_shapes=[pltpu.SMEM((requests,), jnp.int32)],
        compiler_params=pltpu.CompilerParams(vmem_limit_bytes=4 * MIB),
        name="place_rows",
    )(mine, returned)
    return (out, new_state.reshape(ssm_state.shape), new_conv_x, new_conv_bc)


def solution(mesh):
    in_specs = (
        P("req", None, "head"),
        P(None, None, "head"),
        P(),
        P(None, "head"),
        P(None, "head"),
        P(),
        P("head"),
        P("head"),
        P("head"),
        P("head"),
        P("head", None),
        P("req", "head", None, None),
        P("req", None, "head"),
        P("req", None, None),
        P(),
        P(),
        P(),
    )
    out_specs = (
        P("req", None, "head"),
        P("req", "head", None, None),
        P("req", None, "head"),
        P("req", None, None),
    )
    return jax.shard_map(
        per_device, mesh=mesh, in_specs=in_specs, out_specs=out_specs, check_vma=False
    )
```
